512 devices in a mesh: band: 64 (over x_lo, z, core), tile: 8 (over y, x_hi).
Axes of the slice: x: 4 (x_hi: 2, x_lo: 2; x = x_hi * 2 + x_lo), y: 4, z: 16, core: 2. Of those that a mesh axis runs over, the one named last changes fastest.
Arguments:
- alm: bfloat16 [1024, 9, 2, 1024], P('band', None, None, 'tile'), may hold values from -22 to 22
- legendre: bfloat16 [1024, 1024, 1024], P('band', 'tile'), may hold values from -0.1875 to 0.1875
- order_of_slot: int32 [1024], replicated, may hold values from 0 to 1023, each once
Outputs:
- ilc_map: float32 [1024, 4096], P('band', 'tile')
- ilc_alm: float32 [1024, 2, 1024], P('band', None, 'tile')
The draws below stay inside these ranges and needn't reach their ends.
Inputs may be any that keep to these rules, and one draw needn't show every extreme that they name: `order_of_slot`: every order 0 to 1023 stands in exactly one slot.
All inputs are finite; a program needn't handle non-finite values.
Results may differ from the reference program's by a relative error of at most 0.02.
Values may be sent and summed in bfloat16 or wider, within the bound.
A program may use at most 64 MiB of HBM per device.

```python
import math
import jax
import jax.numpy as jnp
from jax import lax

C = 9
L = 1024
NLON = 4096
HALO = 32
CYCLES = 1024
N_TILE = 8


def draw_alm(key, part):
    subkeys = jax.random.split(key, 4)
    response = jax.random.uniform(subkeys[0], (C,), jnp.float32, 0.6, 1.4)
    noise_level = jnp.exp(jax.random.uniform(subkeys[1], (C,), jnp.float32, math.log(0.3), math.log(3.0)))
    common = jnp.clip(jax.random.normal(subkeys[2], (L, 1, 2, L), jnp.float32), -5.0, 5.0)
    separate = jnp.clip(jax.random.normal(subkeys[3], (L, C, 2, L), jnp.float32), -5.0, 5.0)
    values = response[None, :, None, None] * common + noise_level[None, :, None, None] * separate
    return values.astype(jnp.bfloat16)


def shard_levels(stream_key, shape, cuts, least, high):
    level = 1.0
    for axis_at, blocks in cuts:
        heights = jax.random.uniform(jax.random.fold_in(jax.random.fold_in(stream_key, 6), axis_at), (blocks,), jnp.float32, least / len(cuts), high / len(cuts))
        level = level * jnp.repeat(jnp.exp(heights), shape[axis_at] // blocks).reshape((-1,) + (1,) * (len(shape) - 1 - axis_at))
    return level


def normal_values(stream_key, extent, spread, reach, shards=(), kind=jnp.bfloat16):
    array = spread * jax.random.normal(stream_key, extent, jnp.float32)
    if shards:
        array = array * shard_levels(stream_key, extent, shards, -0.22, 0.18)
    return jnp.clip(array, -reach, reach).astype(kind)


def setup_inputs(seed: int = 0) -> dict:
    keys = jax.random.split(jax.random.key(seed), 4)
    return {
        "alm": draw_alm(jax.random.fold_in(keys[3], 71), 0),
        "legendre": normal_values(keys[1], (L, L, CYCLES), L ** -0.5, 0.1875, ((0, 64), (1, 8))),
        "order_of_slot": jax.random.permutation(keys[2], L).astype(jnp.int32),
    }


RIDGE = 0.1
EPSILON = 1e-06

def make_basis(order_of_slot, begin_at, cell_count):
    columns = begin_at + jnp.arange(cell_count, dtype=jnp.int32)
    phases = order_of_slot[:, None] * columns[None, :] % NLON
    angles = phases.astype(jnp.float32) * (2.0 * math.pi / NLON)
    scaling = 1.0 / math.sqrt(L)
    return jnp.stack([jnp.cos(angles) * scaling, -jnp.sin(angles) * scaling]).astype(jnp.bfloat16)

def pair_table():
    return [(a_at, b_at) for a_at in range(C) for b_at in range(a_at, C)]

def window_sum(products):
    span_cells = products.shape[2]
    width_cells = span_cells - 2 * HALO
    total = products
    span = 1
    while span < 2 * HALO:
        total = total[:, :, :-span] + total[:, :, span:]
        span = span * 2
    return total[:, :, :width_cells] + products[:, :, 2 * HALO:2 * HALO + width_cells]

def smooth_pairs(padded):
    widened = padded.astype(jnp.float32)
    products = jnp.stack([widened[a_at] * widened[b_at] for a_at, b_at in pair_table()])
    return window_sum(products) / (2 * HALO + 1)

def solve_weights(smoothed):
    entries = {}
    for pair_at, (a_at, b_at) in enumerate(pair_table()):
        entries[a_at, b_at] = smoothed[pair_at]
    trace_mean = entries[0, 0]
    for chan_at in range(1, C):
        trace_mean = trace_mean + entries[chan_at, chan_at]
    ridge_term = RIDGE * (trace_mean / C + EPSILON)
    factor = {}
    for row_at in range(C):
        for col_at in range(row_at + 1):
            running = entries[col_at, row_at]
            if row_at == col_at:
                running = running + ridge_term
            for inner_at in range(col_at):
                running = running - factor[row_at, inner_at] * factor[col_at, inner_at]
            if row_at == col_at:
                factor[row_at, row_at] = jnp.sqrt(running)
            else:
                factor[row_at, col_at] = running / factor[col_at, col_at]
    forward = []
    for row_at in range(C):
        running = jnp.ones_like(ridge_term)
        for inner_at in range(row_at):
            running = running - factor[row_at, inner_at] * forward[inner_at]
        forward.append(running / factor[row_at, row_at])
    backward = [forward[0]] * C
    for row_at in reversed(range(C)):
        running = forward[row_at]
        for inner_at in range(row_at + 1, C):
            running = running - factor[inner_at, row_at] * backward[inner_at]
        backward[row_at] = running / factor[row_at, row_at]
    normal = backward[0]
    for chan_at in range(1, C):
        normal = normal + backward[chan_at]
    return jnp.stack([solved / normal for solved in backward])

def low_then_float(values):
    return lax.optimization_barrier(values.astype(jnp.bfloat16)).astype(jnp.float32)

def reference(alm, legendre, order_of_slot):
    cycle_total = legendre.shape[2]
    block_len = L // N_TILE
    cycle_sum = jnp.zeros((L, C, 2, cycle_total), jnp.float32)
    for block_at in range(N_TILE):
        alm_block = lax.slice_in_dim(alm, block_at * block_len, (block_at + 1) * block_len, axis=3).astype(jnp.float32)
        table_block = lax.slice_in_dim(legendre, block_at * block_len, (block_at + 1) * block_len, axis=1).astype(jnp.float32)
        block_term = jnp.einsum('scel,slr->scer', alm_block, table_block)
        cycle_sum = cycle_sum + low_then_float(block_term)
    cycle_modes = low_then_float(cycle_sum)
    basis = make_basis(order_of_slot, 0, NLON).astype(jnp.float32)
    channel_maps = jnp.einsum('scer,esx->crx', cycle_modes, basis).astype(jnp.bfloat16)
    padded = jnp.concatenate([channel_maps[:, :, NLON - HALO:], channel_maps, channel_maps[:, :, :HALO]], axis=2)
    block_cells = 512 if NLON % 512 == 0 else NLON
    pieces = []
    for block_at in range(NLON // block_cells):
        window = lax.slice_in_dim(padded, block_at * block_cells, block_at * block_cells + block_cells + 2 * HALO, axis=2)
        weights = solve_weights(smooth_pairs(window))
        source = lax.slice_in_dim(channel_maps, block_at * block_cells, (block_at + 1) * block_cells, axis=2).astype(jnp.float32)
        pieces.append(lax.optimization_barrier(jnp.sum(weights * source, axis=0)))
    ilc_map = jnp.concatenate(pieces, axis=1)
    map_float = low_then_float(ilc_map)
    cycle_spectra = low_then_float(jnp.einsum('rx,esx->res', map_float, basis))
    outputs = []
    for block_at in range(N_TILE):
        table_block = lax.slice_in_dim(legendre, block_at * block_len, (block_at + 1) * block_len, axis=1).astype(jnp.float32)
        outputs.append(jnp.einsum('slr,res->sel', table_block, cycle_spectra))
    ilc_alm = jnp.concatenate(outputs, axis=2)
    return (ilc_map, ilc_alm)
```

```python
import math

import jax
import jax.numpy as jnp
import numpy as np
from jax import lax
from jax.experimental import pallas as pl
from jax.experimental.pallas import tpu as pltpu
from jax.sharding import PartitionSpec as P

C = 9
HALO = 32
RIDGE = 0.1
EPSILON = 1e-06
NB = 64
NT = 8
F32 = jnp.float32
BF16 = jnp.bfloat16
MESH = pl.DeviceIdType.MESH


def tables():
    xl, j, xs = np.meshgrid(np.arange(8), np.arange(2), np.arange(4), indexing="ij")
    xa, jr = (xl + 8 * xs).reshape(-1), j.reshape(-1)
    m0, m1 = np.arange(128), np.arange(8)
    ang = 2 * np.pi * ((xa[:, None] * m1[None, :]) % 32) / 32
    same = (jr[:, None, None] == np.arange(2)[None, None, :]).astype(np.float64)
    cs, sn = np.cos(ang)[:, :, None] * same, np.sin(ang)[:, :, None] * same
    real = np.stack([cs, -sn], axis=3).reshape(64, 32)
    imag = np.stack([sn, cs], axis=3).reshape(64, 32)
    first = np.concatenate([real, imag], axis=0)
    high = first.astype(BF16).astype(np.float64)
    first = np.concatenate([high, first - high], axis=1)
    ang = 2 * np.pi * (xa[:, None] * m0[None, :]) / 4096
    twiddle = np.stack([np.cos(ang), np.sin(ang)])
    ang = 2 * np.pi * ((m0[:, None] * m0[None, :]) % 128) / 128
    second = np.concatenate([np.cos(ang), -np.sin(ang)], axis=0) / 32
    back = np.concatenate([np.cos(ang), -np.sin(ang)], axis=1) / 32
    ang = 2 * np.pi * ((m1[:, None] * xa[None, :]) % 32) / 32
    same = (np.arange(2)[:, None, None] == jr[None, None, :]).astype(np.float64)
    cs, sn = np.cos(ang)[None] * same, np.sin(ang)[None] * same
    e0 = np.concatenate([cs, sn], axis=2).reshape(16, 128)
    e1 = np.concatenate([-sn, cs], axis=2).reshape(16, 128)
    last = np.concatenate([e0, e1], axis=0)
    return (
        first.astype(BF16),
        twiddle.astype(np.float32),
        second.astype(BF16),
        back.astype(BF16),
        last.astype(BF16),
    )


def pair_table():
    return [(a, b) for a in range(C) for b in range(a, C)]


def window_sums(maps, smoothed):
    sub = lax.broadcasted_iota(jnp.int32, (8, 128), 0) % 4
    below = [jnp.where(sub >= k, 1.0, 0.0).astype(F32) for k in (1, 2, 3)]
    above = [jnp.where(sub <= 3 - k, 1.0, 0.0).astype(F32) for k in (1, 2, 3)]
    for at, (a, b) in enumerate(pair_table()):
        prod = [
            maps[a, 8 * i : 8 * i + 8, :] * maps[b, 8 * i : 8 * i + 8, :] for i in range(8)
        ]
        pre, post = [prod[0]], [prod[7]]
        for i in range(1, 8):
            pre.append(pre[-1] + prod[i])
            post.append(post[-1] + prod[7 - i])
        post = post[::-1]
        seg = pre[7]
        low = high = None
        for k in (1, 2, 3):
            down = below[k - 1] * pltpu.roll(seg, k, 0)
            up = above[k - 1] * pltpu.roll(seg, 8 - k, 0)
            low = down if low is None else low + down
            high = up if high is None else high + up
        total = seg + low + high
        for i in range(8):
            before = pltpu.roll(post[i] + high, 1, 1)
            after = pltpu.roll(pre[i] + low, 127, 1)
            smoothed[at, 8 * i : 8 * i + 8, :] = (before + total + after) * (
                1.0 / (2 * HALO + 1)
            )


def solve_cells(maps, smoothed, out):
    index = {}
    for at, (a, b) in enumerate(pair_table()):
        index[a, b] = at

    def step(i, _):
        rows = pl.ds(pl.multiple_of(i * 8, 8), 8)
        left = {key: smoothed[at, rows, :] for key, at in index.items()}
        trace = left[0, 0]
        for c in range(1, C):
            trace = trace + left[c, c]
        ridge = RIDGE * (trace * (1.0 / C) + EPSILON)
        for c in range(C):
            left[c, c] = left[c, c] + ridge
        ones = [jnp.ones((8, 128), F32) for _ in range(C)]
        vals = [maps[c, rows, :] for c in range(C)]
        top = bottom = None
        for k in range(C):
            inverse = 1.0 / left[k, k]
            scaled = ones[k] * inverse
            add_b, add_t = scaled * ones[k], scaled * vals[k]
            bottom = add_b if bottom is None else bottom + add_b
            top = add_t if top is None else top + add_t
            for r in range(k + 1, C):
                ratio = left[k, r] * inverse
                for q in range(r, C):
                    left[r, q] = left[r, q] - ratio * left[k, q]
                ones[r] = ones[r] - ratio * ones[k]
                vals[r] = vals[r] - ratio * vals[k]
        out[rows, :] = top / bottom
        return 0

    lax.fori_loop(0, 8, step, 0)


def turn(block):
    return jnp.transpose(block, (1, 0))


def kernel(
    alm_h, leg_h, ord_h, first_h, twid_h, second_h, back_h, last_h,
    map_o, alm_o,
    alm_v, leg_v, ord_v, first, twid, second, back, last,
    stage, parts, heard, slot_s, slot_r, turned, modes, gathered, to_order, to_slot,
    maps, smoothed, ilc, cells, cells_r, spec, spec_s, spec_r, spec_t, every,
    load_sem, send_sem, recv_sem,
):
    b = lax.axis_index("band")
    t = lax.axis_index("tile")
    owner_band = 8 * t + lax.div(b, 8)
    lane = lax.broadcasted_iota(jnp.int32, (8, 128), 1)

    loads = []
    for at, (src, dst) in enumerate(
        [(alm_h, alm_v)]
        + [(leg_h.at[pl.ds(4 * k, 4)], leg_v.at[pl.ds(4 * k, 4)]) for k in range(4)]
        + [(ord_h, ord_v), (first_h, first), (twid_h, twid), (second_h, second)]
        + [(back_h, back), (last_h, last)]
    ):
        copy = pltpu.make_async_copy(src, dst, load_sem.at[at])
        copy.start()
        loads.append(copy)

    bar = pltpu.get_barrier_semaphore()

    def greet_band(d, _):
        pl.semaphore_signal(
            bar, inc=1, device_id={"band": lax.rem(b + d, NB), "tile": t}, device_id_type=MESH
        )
        return 0

    lax.fori_loop(1, NB, greet_band, 0)
    for d in range(1, NT):
        pl.semaphore_signal(
            bar, inc=1, device_id={"band": b, "tile": lax.rem(t + d, NT)}, device_id_type=MESH
        )
    source_tile = lax.div(b, 8)
    for k in range(8):
        source_band = 8 * lax.rem(b, 8) + k
        own = jnp.logical_and(source_band == b, source_tile == t)

        @pl.when(jnp.logical_not(own))
        def _():
            pl.semaphore_signal(
                bar, inc=1, device_id={"band": source_band, "tile": source_tile},
                device_id_type=MESH,
            )

    loads[0].wait()
    for k in range(4):
        loads[1 + k].wait()
        for s in range(4 * k, 4 * k + 4):
            left = alm_v[s].reshape(18, 128)
            out = jnp.dot(left, leg_v[s], preferred_element_type=F32)
            for q in range(NT):
                stage[q, pl.ds(s, 18, stride=16), :] = out[:, 128 * q : 128 * q + 128]
    for q in range(NT):
        parts[q] = stage[q].astype(BF16)

    pl.semaphore_wait(bar, 78 - jnp.where(owner_band == b, 1, 0))

    for d in range(1, NT):
        other = lax.rem(t + d, NT)
        pltpu.make_async_remote_copy(
            src_ref=parts.at[other], dst_ref=heard.at[t], send_sem=send_sem.at[0],
            recv_sem=recv_sem.at[0], device_id={"band": b, "tile": other}, device_id_type=MESH,
        ).start()
    pltpu.make_async_copy(parts.at[t], heard.at[t], recv_sem.at[0]).start()

    for copy in loads[5:]:
        copy.wait()
    orders = ord_v[...].astype(F32)
    cols = turn(jnp.concatenate([orders, jnp.zeros((120, 128), F32)], axis=0))
    turned[0:128, :] = cols
    wide = lax.broadcasted_iota(jnp.int32, (8, 1024), 1).astype(F32)
    for s in range(16):
        pick = turned[pl.ds(s, 8, stride=16), :]
        for h in range(0, 8, 2):
            rows = [
                jnp.where(pick[:, k : k + 1] == wide, 1.0, 0.0) for k in (h, h + 1)
            ]
            to_order[s * 64 + h * 8 : s * 64 + h * 8 + 16, :] = jnp.concatenate(
                rows, axis=0
            ).astype(BF16)
    tall = lax.broadcasted_iota(jnp.int32, (128, 128), 0).astype(F32)
    for h in range(8):
        row = jnp.broadcast_to(orders[h : h + 1, :], (128, 128))
        for k in range(8):
            to_slot[128 * k : 128 * k + 128, 128 * h : 128 * h + 128] = jnp.where(
                row == tall + 128.0 * k, 1.0, 0.0
            ).astype(BF16)

    pltpu.make_async_copy(heard, heard, recv_sem.at[0]).wait()
    total = heard[0].astype(F32)
    for q in range(1, NT):
        total = total + heard[q].astype(F32)
    total = jnp.concatenate([total, jnp.zeros((96, 128), F32)], axis=0)
    for k in range(3):
        block = turn(total[128 * k : 128 * k + 128])
        slot_s[:, k] = block.astype(BF16).reshape(NB, 2, 128)

    def send_slots(d, _):
        other = lax.rem(b + d, NB)
        pltpu.make_async_remote_copy(
            src_ref=slot_s.at[other], dst_ref=slot_r.at[b], send_sem=send_sem.at[1],
            recv_sem=recv_sem.at[1], device_id={"band": other, "tile": t}, device_id_type=MESH,
        ).start()
        return 0

    lax.fori_loop(1, NB, send_slots, 0)
    pltpu.make_async_copy(slot_s.at[b], slot_r.at[b], recv_sem.at[1]).start()
    pltpu.make_async_copy(slot_r, slot_r, recv_sem.at[1]).wait()

    for k in range(3):
        block = slot_r[:, k].astype(F32)
        block = jnp.concatenate([block[:, 0, :], block[:, 1, :]], axis=0)
        turned[128 * k : 128 * k + 128, :] = turn(block)
    lane24 = lax.broadcasted_iota(jnp.int32, (24, 128), 1)
    pieces = []
    for p in range(8):
        even = turned[pl.ds(2 * p, 24, stride=16), :]
        odd = turned[pl.ds(2 * p + 1, 24, stride=16), :]
        first_r = jnp.where(lane24 < 64, even, pltpu.roll(odd, 64, 1))
        second_r = jnp.where(lane24 < 64, pltpu.roll(even, 64, 1), odd)
        pieces.append(jnp.concatenate([first_r, second_r], axis=0).astype(BF16))
    ordered = jnp.dot(
        jnp.concatenate(pieces, axis=1), to_order[...], preferred_element_type=F32
    )
    for k in range(8):
        modes[k] = ordered[:, 128 * k : 128 * k + 128]
    for c in range(C):
        for k in range(8):
            gathered[c, 4 * k : 4 * k + 2, :] = modes[k, 2 * c : 2 * c + 2, :]
            gathered[c, 4 * k + 2 : 4 * k + 4, :] = modes[k, 24 + 2 * c : 26 + 2 * c, :]

    twr, twi = twid[0], twid[1]
    for c in range(C):
        data = gathered[c].astype(BF16)
        grid = jnp.dot(
            first[...], jnp.concatenate([data, data], axis=0), preferred_element_type=F32
        )
        re, im = grid[:64], grid[64:]
        both = jnp.concatenate([re * twr - im * twi, re * twi + im * twr], axis=1)
        maps[c] = (
            jnp.dot(both.astype(BF16), second[...], preferred_element_type=F32)
            .astype(BF16)
            .astype(F32)
        )

    window_sums(maps, smoothed)
    solve_cells(maps, smoothed, ilc)

    grid = jnp.dot(ilc[...].astype(BF16), back[...], preferred_element_type=F32)
    re, im = grid[:, :128], grid[:, 128:]
    both = jnp.concatenate([re * twr + im * twi, im * twr - re * twi], axis=0)
    spec[...] = jnp.dot(last[...], both.astype(BF16), preferred_element_type=F32)
    flat = jnp.concatenate([spec[pl.ds(k, 4, stride=8), :] for k in range(8)], axis=1)
    flat = jnp.concatenate([flat, jnp.zeros((4, 1024), F32)], axis=0)
    placed = jnp.dot(flat.astype(BF16), to_slot[...], preferred_element_type=F32)
    for k in range(8):
        spec_s[k] = placed[0:4, 128 * k : 128 * k + 128].astype(BF16)

    def send_spectra(d, _):
        other = lax.rem(b + d, NB)
        pltpu.make_async_remote_copy(
            src_ref=spec_s.at[lax.div(other, 8)], dst_ref=spec_r.at[b], send_sem=send_sem.at[2],
            recv_sem=recv_sem.at[2], device_id={"band": other, "tile": t}, device_id_type=MESH,
        ).start()
        return 0

    lax.fori_loop(1, NB, send_spectra, 0)
    pltpu.make_async_copy(spec_s.at[lax.div(b, 8)], spec_r.at[b], recv_sem.at[2]).start()

    lines = jnp.concatenate(
        [ilc[pl.ds(k, 8, stride=8), :] for k in range(8)] + [jnp.zeros((64, 128), F32)], axis=0
    )
    turned[0:128, :] = turn(lines)
    lane32 = lax.broadcasted_iota(jnp.int32, (32, 128), 1)
    for j in range(2):
        line = None
        for k in range(4):
            part = turned[pl.ds(k, 32, stride=4), :]
            part = pltpu.roll(part, (32 * k - 32 * j) % 128, 1) if k != j else part
            keep = jnp.logical_and(lane32 >= 32 * k, lane32 < 32 * k + 32)
            part = jnp.where(keep, part, 0.0)
            line = part if line is None else line + part
        cells[pl.ds(j, 32, stride=2), :] = line
    place = pl.ds(pl.multiple_of(8 * lax.rem(b, 8), 8), 8)
    for q in range(NT):
        own = jnp.logical_and(owner_band == b, t == q)

        @pl.when(own)
        def _():
            pltpu.make_async_copy(
                cells.at[8 * q : 8 * q + 8], cells_r.at[place], recv_sem.at[4]
            ).start()

        @pl.when(jnp.logical_not(own))
        def _():
            pltpu.make_async_remote_copy(
                src_ref=cells.at[8 * q : 8 * q + 8], dst_ref=cells_r.at[place],
                send_sem=send_sem.at[4], recv_sem=recv_sem.at[4],
                device_id={"band": owner_band, "tile": q}, device_id_type=MESH,
            ).start()

    pltpu.make_async_copy(spec_r, spec_r, recv_sem.at[2]).wait()
    start = pl.multiple_of(16 * lax.rem(b, 8), 16)
    block = spec_r[...].astype(F32)
    for e in range(2):
        spec_t[e] = turn(block[:, 2 * e : 2 * e + 2, :].reshape(128, 128))
    own_s = [spec_t[e, pl.ds(start, 16), :] for e in range(2)]
    every[t] = jnp.concatenate(own_s, axis=0).astype(BF16)
    for d in range(1, NT):
        other = lax.rem(t + d, NT)
        pltpu.make_async_remote_copy(
            src_ref=every.at[t], dst_ref=every.at[t], send_sem=send_sem.at[3],
            recv_sem=recv_sem.at[3], device_id={"band": b, "tile": other}, device_id_type=MESH,
        ).start()
    seven = every.at[pl.ds(0, NT - 1)]
    pltpu.make_async_copy(seven, seven, recv_sem.at[3]).wait()
    full = jnp.concatenate([every[q] for q in range(NT)], axis=1)
    for s in range(16):
        out = lax.dot_general(
            full, leg_v[s], (((1,), (1,)), ((), ())), preferred_element_type=F32
        )
        alm_o[s, 0:1, :] = out[s : s + 1]
        alm_o[s, 1:2, :] = out[16 + s : 17 + s]

    pltpu.make_async_copy(cells_r, cells_r, recv_sem.at[4]).wait()
    for q in range(4):
        for j in range(2):
            ilc[pl.ds(16 * q + j, 8, stride=2), :] = cells_r[pl.ds(2 * q + j, 8, stride=8), :]
        map_o[:, 128 * q : 128 * q + 128] = ilc[16 * q : 16 * q + 16, :]

    sent = parts.at[pl.ds(0, NT - 1)]
    pltpu.make_async_copy(sent, sent, send_sem.at[0]).wait()
    sent = slot_s.at[pl.ds(0, NB - 1)]
    pltpu.make_async_copy(sent, sent, send_sem.at[1]).wait()
    sent = spec_r.at[pl.ds(0, NB - 1)]
    pltpu.make_async_copy(sent, sent, send_sem.at[2]).wait()
    pltpu.make_async_copy(seven, seven, send_sem.at[3]).wait()
    mine = owner_band == b

    @pl.when(mine)
    def _():
        sent = cells.at[0:56]
        pltpu.make_async_copy(sent, sent, send_sem.at[4]).wait()

    @pl.when(jnp.logical_not(mine))
    def _():
        pltpu.make_async_copy(cells, cells, send_sem.at[4]).wait()


def body(alm, legendre, order_of_slot):
    any_space = pl.BlockSpec(memory_space=pl.ANY)
    vmem = pl.BlockSpec(memory_space=pltpu.VMEM)
    first, twid, second, back, last = tables()
    scratch = [
        ((16, C, 2, 128), BF16),
        ((16, 128, 1024), BF16),
        ((8, 128), jnp.int32),
        (first.shape, BF16),
        (twid.shape, F32),
        (second.shape, BF16),
        (back.shape, BF16),
        (last.shape, BF16),
        ((NT, 288, 128), F32),
        ((NT, 288, 128), BF16),
        ((NT, 288, 128), BF16),
        ((NB, 3, 2, 128), BF16),
        ((NB, 3, 2, 128), BF16),
        ((384, 128), F32),
        ((8, 48, 128), F32),
        ((C, 32, 128), F32),
        ((1024, 1024), BF16),
        ((1024, 1024), BF16),
        ((C, 64, 128), F32),
        ((45, 64, 128), F32),
        ((64, 128), F32),
        ((64, 128), F32),
        ((64, 128), F32),
        ((32, 128), F32),
        ((8, 4, 128), BF16),
        ((NB, 4, 128), BF16),
        ((2, 128, 128), F32),
        ((NT, 32, 128), BF16),
    ]
    return pl.pallas_call(
        kernel,
        out_shape=(
            jax.ShapeDtypeStruct((16, 512), F32),
            jax.ShapeDtypeStruct((16, 2, 128), F32),
        ),
        in_specs=[any_space] * 8,
        out_specs=(vmem, vmem),
        scratch_shapes=[pltpu.VMEM(shape, kind) for shape, kind in scratch]
        + [
            pltpu.SemaphoreType.DMA((11,)),
            pltpu.SemaphoreType.DMA((5,)),
            pltpu.SemaphoreType.DMA((5,)),
        ],
        compiler_params=pltpu.CompilerParams(
            collective_id=0, has_side_effects=True, vmem_limit_bytes=48 * 1024 * 1024
        ),
    )(alm, legendre, order_of_slot.reshape(8, 128), first, twid, second, back, last)


def solution(mesh):
    placed = (P("band", None, None, "tile"), P("band", "tile", None), P())
    return jax.shard_map(
        body,
        mesh=mesh,
        in_specs=placed,
        out_specs=(P("band", "tile"), P("band", None, "tile")),
        check_vma=False,
    )
```

```python
import math

import jax
import jax.numpy as jnp
import numpy as np
from jax import lax
from jax.experimental import pallas as pl
from jax.experimental.pallas import tpu as pltpu
from jax.sharding import PartitionSpec as P

C = 9
HALO = 32
RIDGE = 0.1
EPSILON = 1e-06
NB = 64
NT = 8
F32 = jnp.float32
BF16 = jnp.bfloat16
MESH = pl.DeviceIdType.MESH


SCRATCH = {
    "alm_v": ((16, C, 2, 128), BF16),
    "leg_v": ((16, 128, 1024), BF16),
    "ord_v": ((8, 128), jnp.int32),
    "first": ((128, 64), BF16),
    "twid": ((2, 64, 128), F32),
    "second": ((256, 128), BF16),
    "back": ((128, 256), BF16),
    "last": ((128, 128), BF16),
    "stage": ((NT, 288, 128), F32),
    "parts": ((NT, 288, 128), BF16),
    "heard": ((NT, 288, 128), BF16),
    "slot_s": ((NB, 3, 2, 128), BF16),
    "slot_r": ((NB, 3, 2, 128), BF16),
    "turned": ((384, 128), F32),
    "modes": ((8, 48, 128), F32),
    "gathered": ((C, 32, 128), F32),
    "to_order": ((1024, 1024), BF16),
    "to_slot": ((1024, 1024), BF16),
    "maps": ((C, 64, 128), F32),
    "smoothed": ((45, 64, 128), F32),
    "ilc": ((64, 128), F32),
    "cells": ((64, 128), F32),
    "cells_r": ((64, 128), F32),
    "spec": ((128, 128), F32),
    "spec_s": ((16, 2, 128), BF16),
    "spec_r": ((NB, 2, 128), BF16),
    "spec_t": ((128, 128), F32),
    "every": ((NT, 32, 128), BF16),
    "sums": ((16, 32, 128), F32),
}


def scratch_list():
    return [pltpu.VMEM(shape, kind) for shape, kind in SCRATCH.values()]


def tables():
    xl, j, xs = np.meshgrid(np.arange(8), np.arange(2), np.arange(4), indexing="ij")
    xa, jr = (xl + 8 * xs).reshape(-1), j.reshape(-1)
    m0, m1 = np.arange(128), np.arange(8)
    ang = 2 * np.pi * ((xa[:, None] * m1[None, :]) % 32) / 32
    same = (jr[:, None, None] == np.arange(2)[None, None, :]).astype(np.float64)
    cs, sn = np.cos(ang)[:, :, None] * same, np.sin(ang)[:, :, None] * same
    real = np.stack([cs, -sn], axis=3).reshape(64, 32)
    imag = np.stack([sn, cs], axis=3).reshape(64, 32)
    first = np.concatenate([real, imag], axis=0)
    high = first.astype(BF16).astype(np.float64)
    first = np.concatenate([high, first - high], axis=1)
    ang = 2 * np.pi * (xa[:, None] * m0[None, :]) / 4096
    twiddle = np.stack([np.cos(ang), np.sin(ang)])
    ang = 2 * np.pi * ((m0[:, None] * m0[None, :]) % 128) / 128
    second = np.concatenate([np.cos(ang), -np.sin(ang)], axis=0) / 32
    back = np.concatenate([np.cos(ang), -np.sin(ang)], axis=1) / 32
    ang = 2 * np.pi * ((m1[:, None] * xa[None, :]) % 32) / 32
    same = (np.arange(2)[:, None, None] == jr[None, None, :]).astype(np.float64)
    cs, sn = np.cos(ang)[None] * same, np.sin(ang)[None] * same
    e0 = np.concatenate([cs, sn], axis=2).reshape(16, 128)
    e1 = np.concatenate([-sn, cs], axis=2).reshape(16, 128)
    none = np.zeros((48, 128))
    last = np.concatenate([e0, none, e1, none], axis=0)
    return (
        first.astype(BF16),
        twiddle.astype(np.float32),
        second.astype(BF16),
        back.astype(BF16),
        last.astype(BF16),
    )


def pair_table():
    return [(a, b) for a in range(C) for b in range(a, C)]


def window_sums(maps, smoothed):
    sub = lax.broadcasted_iota(jnp.int32, (8, 128), 0) % 4
    below = [jnp.where(sub >= k, 1.0, 0.0).astype(F32) for k in (1, 2, 3)]
    above = [jnp.where(sub <= 3 - k, 1.0, 0.0).astype(F32) for k in (1, 2, 3)]
    for at, (a, b) in enumerate(pair_table()):
        prod = [
            maps[a, 8 * i : 8 * i + 8, :] * maps[b, 8 * i : 8 * i + 8, :] for i in range(8)
        ]
        pre, post = [prod[0]], [prod[7]]
        for i in range(1, 8):
            pre.append(pre[-1] + prod[i])
            post.append(post[-1] + prod[7 - i])
        post = post[::-1]
        seg = pre[7]
        low = high = None
        for k in (1, 2, 3):
            down = below[k - 1] * pltpu.roll(seg, k, 0)
            up = above[k - 1] * pltpu.roll(seg, 8 - k, 0)
            low = down if low is None else low + down
            high = up if high is None else high + up
        total = seg + low + high
        for i in range(8):
            before = pltpu.roll(post[i] + high, 1, 1)
            after = pltpu.roll(pre[i] + low, 127, 1)
            smoothed[at, 8 * i : 8 * i + 8, :] = (before + total + after) * (
                1.0 / (2 * HALO + 1)
            )


def solve_cells(maps, smoothed, out):
    index = {}
    for at, (a, b) in enumerate(pair_table()):
        index[a, b] = at

    def step(i, _):
        rows = pl.ds(pl.multiple_of(i * 8, 8), 8)
        left = {key: smoothed[at, rows, :] for key, at in index.items()}
        trace = left[0, 0]
        for c in range(1, C):
            trace = trace + left[c, c]
        ridge = RIDGE * (trace * (1.0 / C) + EPSILON)
        for c in range(C):
            left[c, c] = left[c, c] + ridge
        ones = [jnp.ones((8, 128), F32) for _ in range(C)]
        vals = [maps[c, rows, :] for c in range(C)]
        top = bottom = None
        for k in range(C):
            inverse = 1.0 / left[k, k]
            scaled = ones[k] * inverse
            add_b, add_t = scaled * ones[k], scaled * vals[k]
            bottom = add_b if bottom is None else bottom + add_b
            top = add_t if top is None else top + add_t
            for r in range(k + 1, C):
                ratio = left[k, r] * inverse
                for q in range(r, C):
                    left[r, q] = left[r, q] - ratio * left[k, q]
                ones[r] = ones[r] - ratio * ones[k]
                vals[r] = vals[r] - ratio * vals[k]
        out[rows, :] = top / bottom
        return 0

    lax.fori_loop(0, 8, step, 0)


def band_peer(d, b):
    k, i = lax.div(d, 4), lax.rem(d, 4)
    dz = lax.rem(24 + (1 - 2 * lax.rem(k, 2)) * lax.div(k + 1, 2), 16)
    x = lax.rem(lax.div(b, 32) + lax.div(i, 2) + 1, 2)
    z = lax.rem(lax.rem(lax.div(b, 2), 16) + dz, 16)
    core = lax.rem(lax.rem(b, 2) + lax.rem(i, 2) + 1, 2)
    return (x * 16 + z) * 2 + core


FAR_FIRST = ((2, 1), (1, 1), (3, 1), (2, 0), (0, 1), (1, 0), (3, 0))


def tile_peer(t, dy, dx):
    return 2 * lax.rem(lax.div(t, 2) + dy, 4) + lax.rem(lax.rem(t, 2) + dx, 2)


def turn(block):
    return jnp.transpose(block, (1, 0))


def kernel(
    alm_h, leg_h, ord_h, first_h, twid_h, second_h, back_h, last_h,
    map_o, alm_o,
    alm_v, leg_v, ord_v, first, twid, second, back, last,
    stage, parts, heard, slot_s, slot_r, turned, modes, gathered, to_order, to_slot,
    maps, smoothed, ilc, cells, cells_r, spec, spec_s, spec_r, spec_t, every, sums,
    load_sem, send_sem, recv_sem, tile_sem,
):
    b = lax.axis_index("band")
    t = lax.axis_index("tile")
    owner_band = 8 * t + lax.div(b, 8)
    lane = lax.broadcasted_iota(jnp.int32, (8, 128), 1)

    loads = []
    for at, (src, dst) in enumerate(
        [(alm_h, alm_v)]
        + [(leg_h.at[pl.ds(4 * k, 4)], leg_v.at[pl.ds(4 * k, 4)]) for k in range(4)]
        + [(ord_h, ord_v), (first_h, first), (twid_h, twid), (second_h, second)]
        + [(back_h, back), (last_h, last)]
    ):
        copy = pltpu.make_async_copy(src, dst, load_sem.at[at])
        copy.start()
        loads.append(copy)

    bar = pltpu.get_barrier_semaphore()

    def greet_band(d, _):
        pl.semaphore_signal(
            bar, inc=1, device_id={"band": band_peer(d, b), "tile": t}, device_id_type=MESH
        )
        return 0

    lax.fori_loop(0, NB - 1, greet_band, 0)
    for d in range(1, NT):
        pl.semaphore_signal(
            bar, inc=1, device_id={"band": b, "tile": lax.rem(t + d, NT)}, device_id_type=MESH
        )

    loads[0].wait()
    for k in range(4):
        loads[1 + k].wait()
        for s in range(4 * k, 4 * k + 4):
            left = alm_v[s].reshape(18, 128)
            out = jnp.dot(left, leg_v[s], preferred_element_type=F32)
            for q in range(NT):
                stage[q, pl.ds(s, 18, stride=16), :] = out[:, 128 * q : 128 * q + 128]
    for q in range(NT):
        parts[q] = stage[q].astype(BF16)

    pl.semaphore_wait(bar, 70)

    for dy, dx in FAR_FIRST:
        other = tile_peer(t, dy, dx)
        pltpu.make_async_remote_copy(
            src_ref=parts.at[other], dst_ref=heard.at[t], send_sem=send_sem.at[0],
            recv_sem=recv_sem.at[0], device_id={"band": b, "tile": other}, device_id_type=MESH,
        ).start()
    pltpu.make_async_copy(parts.at[t], heard.at[t], recv_sem.at[0]).start()

    for copy in loads[5:]:
        copy.wait()
    orders = ord_v[...].astype(F32)
    cols = turn(jnp.concatenate([orders, jnp.zeros((120, 128), F32)], axis=0))
    turned[0:128, :] = cols
    wide = lax.broadcasted_iota(jnp.int32, (8, 1024), 1).astype(F32)
    for s in range(16):
        pick = turned[pl.ds(s, 8, stride=16), :]
        for h in range(0, 8, 2):
            rows = [
                jnp.where(pick[:, k : k + 1] == wide, 1.0, 0.0) for k in (h, h + 1)
            ]
            to_order[s * 64 + h * 8 : s * 64 + h * 8 + 16, :] = jnp.concatenate(
                rows, axis=0
            ).astype(BF16)
    tall = lax.broadcasted_iota(jnp.int32, (128, 128), 0).astype(F32)
    for h in range(8):
        row = jnp.broadcast_to(orders[h : h + 1, :], (128, 128))
        for k in range(8):
            to_slot[128 * k : 128 * k + 128, 128 * h : 128 * h + 128] = jnp.where(
                row == tall + 128.0 * k, 1.0, 0.0
            ).astype(BF16)

    pltpu.make_async_copy(heard, heard, recv_sem.at[0]).wait()
    total = heard[0].astype(F32)
    for q in range(1, NT):
        total = total + heard[q].astype(F32)
    total = jnp.concatenate([total, jnp.zeros((96, 128), F32)], axis=0)
    for k in range(3):
        block = turn(total[128 * k : 128 * k + 128])
        slot_s[:, k] = block.astype(BF16).reshape(NB, 2, 128)

    def send_slots(d, _):
        other = band_peer(d, b)
        pltpu.make_async_remote_copy(
            src_ref=slot_s.at[other], dst_ref=slot_r.at[b], send_sem=send_sem.at[1],
            recv_sem=recv_sem.at[1], device_id={"band": other, "tile": t}, device_id_type=MESH,
        ).start()
        return 0

    lax.fori_loop(0, NB - 1, send_slots, 0)
    pltpu.make_async_copy(slot_s.at[b], slot_r.at[b], recv_sem.at[1]).start()
    pltpu.make_async_copy(slot_r, slot_r, recv_sem.at[1]).wait()

    for k in range(3):
        block = slot_r[:, k].astype(F32)
        block = jnp.concatenate([block[:, 0, :], block[:, 1, :]], axis=0)
        turned[128 * k : 128 * k + 128, :] = turn(block)
    lane24 = lax.broadcasted_iota(jnp.int32, (24, 128), 1)
    pieces = []
    for p in range(8):
        even = turned[pl.ds(2 * p, 24, stride=16), :]
        odd = turned[pl.ds(2 * p + 1, 24, stride=16), :]
        first_r = jnp.where(lane24 < 64, even, pltpu.roll(odd, 64, 1))
        second_r = jnp.where(lane24 < 64, pltpu.roll(even, 64, 1), odd)
        pieces.append(jnp.concatenate([first_r, second_r], axis=0).astype(BF16))
    ordered = jnp.dot(
        jnp.concatenate(pieces, axis=1), to_order[...], preferred_element_type=F32
    )
    for k in range(8):
        modes[k] = ordered[:, 128 * k : 128 * k + 128]
    for c in range(C):
        for k in range(8):
            gathered[c, 4 * k : 4 * k + 2, :] = modes[k, 2 * c : 2 * c + 2, :]
            gathered[c, 4 * k + 2 : 4 * k + 4, :] = modes[k, 24 + 2 * c : 26 + 2 * c, :]

    twr, twi = twid[0], twid[1]
    for c in range(C):
        data = gathered[c].astype(BF16)
        grid = jnp.dot(
            first[...], jnp.concatenate([data, data], axis=0), preferred_element_type=F32
        )
        re, im = grid[:64], grid[64:]
        both = jnp.concatenate([re * twr - im * twi, re * twi + im * twr], axis=1)
        maps[c] = (
            jnp.dot(both.astype(BF16), second[...], preferred_element_type=F32)
            .astype(BF16)
            .astype(F32)
        )

    window_sums(maps, smoothed)
    solve_cells(maps, smoothed, ilc)

    twr, twi = twid[0], twid[1]
    grid = jnp.dot(ilc[...].astype(BF16), back[...], preferred_element_type=F32)
    re, im = grid[:, :128], grid[:, 128:]
    both = jnp.concatenate([re * twr + im * twi, im * twr - re * twi], axis=0)
    spec[...] = jnp.dot(last[...], both.astype(BF16), preferred_element_type=F32)
    flat = jnp.concatenate([spec[pl.ds(k, 16, stride=8), :] for k in range(8)], axis=1)
    placed = jnp.dot(flat.astype(BF16), to_slot[...], preferred_element_type=F32)
    half = lax.broadcasted_iota(jnp.int32, (8, 128), 1) < 64
    for k in range(8):
        e0, e1 = (placed[8 * e : 8 * e + 8, 128 * k : 128 * k + 128] for e in range(2))
        low = jnp.where(half, e0, pltpu.roll(e1, 64, 1))
        high = jnp.where(half, pltpu.roll(e0, 64, 1), e1)
        spec_s[2 * k] = low[0:2].astype(BF16)
        spec_s[2 * k + 1] = high[0:2].astype(BF16)
    def send_spectra(d, _):
        other = band_peer(d, b)
        pltpu.make_async_remote_copy(
            src_ref=spec_s.at[lax.div(other, 4)], dst_ref=spec_r.at[b], send_sem=send_sem.at[2],
            recv_sem=recv_sem.at[2], device_id={"band": other, "tile": t}, device_id_type=MESH,
        ).start()
        return 0

    lax.fori_loop(0, NB - 1, send_spectra, 0)
    pltpu.make_async_copy(spec_s.at[lax.div(b, 4)], spec_r.at[b], recv_sem.at[2]).start()

    lines = jnp.concatenate(
        [ilc[pl.ds(k, 8, stride=8), :] for k in range(8)] + [jnp.zeros((64, 128), F32)], axis=0
    )
    turned[0:128, :] = turn(lines)
    lane32 = lax.broadcasted_iota(jnp.int32, (32, 128), 1)
    for j in range(2):
        line = None
        for k in range(4):
            part = turned[pl.ds(k, 32, stride=4), :]
            part = pltpu.roll(part, (32 * k - 32 * j) % 128, 1) if k != j else part
            keep = jnp.logical_and(lane32 >= 32 * k, lane32 < 32 * k + 32)
            part = jnp.where(keep, part, 0.0)
            line = part if line is None else line + part
        cells[pl.ds(j, 32, stride=2), :] = line
    place = pl.ds(pl.multiple_of(8 * lax.rem(b, 8), 8), 8)
    for q in range(NT):
        own = jnp.logical_and(owner_band == b, t == q)

        @pl.when(own)
        def _():
            pltpu.make_async_copy(
                cells.at[8 * q : 8 * q + 8], cells_r.at[place], recv_sem.at[4]
            ).start()

        @pl.when(jnp.logical_not(own))
        def _():
            pltpu.make_async_remote_copy(
                src_ref=cells.at[8 * q : 8 * q + 8], dst_ref=cells_r.at[place],
                send_sem=send_sem.at[4], recv_sem=recv_sem.at[4],
                device_id={"band": owner_band, "tile": q}, device_id_type=MESH,
            ).start()

    pltpu.make_async_copy(spec_r, spec_r, recv_sem.at[2]).wait()
    spec_t[...] = turn(spec_r[...].astype(F32).reshape(128, 128))
    start = 16 * lax.rem(b, 4)
    own_s = [spec_t[pl.ds(pl.multiple_of(64 * e + start, 16), 16), :] for e in range(2)]
    every[t] = jnp.concatenate(own_s, axis=0).astype(BF16)
    for dy, dx in FAR_FIRST:
        other = tile_peer(t, dy, dx)
        pltpu.make_async_remote_copy(
            src_ref=every.at[t], dst_ref=every.at[t], send_sem=send_sem.at[3],
            recv_sem=tile_sem.at[t], device_id={"band": b, "tile": other}, device_id_type=MESH,
        ).start()
    for at, (dy, dx) in enumerate(((0, 0),) + FAR_FIRST[::-1]):
        other = tile_peer(t, dy, dx)
        if at:
            pltpu.make_async_copy(every.at[other], every.at[other], tile_sem.at[other]).wait()
        block = every[other]
        cycles = pl.ds(pl.multiple_of(128 * other, 128), 128)
        for s in range(16):
            out = lax.dot_general(
                block, leg_v[s, :, cycles], (((1,), (1,)), ((), ())), preferred_element_type=F32
            )
            if at == 0:
                sums[s] = out
            elif at < NT - 1:
                sums[s] += out
            else:
                out = out + sums[s]
                alm_o[s, 0:1, :] = out[s : s + 1]
                alm_o[s, 1:2, :] = out[16 + s : 17 + s]

    pltpu.make_async_copy(cells_r, cells_r, recv_sem.at[4]).wait()
    for q in range(4):
        for j in range(2):
            ilc[pl.ds(16 * q + j, 8, stride=2), :] = cells_r[pl.ds(2 * q + j, 8, stride=8), :]
        map_o[:, 128 * q : 128 * q + 128] = ilc[16 * q : 16 * q + 16, :]

    sent = parts.at[pl.ds(0, NT - 1)]
    pltpu.make_async_copy(sent, sent, send_sem.at[0]).wait()
    sent = slot_s.at[pl.ds(0, NB - 1)]
    pltpu.make_async_copy(sent, sent, send_sem.at[1]).wait()
    sent = spec_r.at[pl.ds(0, NB - 1)]
    pltpu.make_async_copy(sent, sent, send_sem.at[2]).wait()
    sent = every.at[pl.ds(0, NT - 1)]
    pltpu.make_async_copy(sent, sent, send_sem.at[3]).wait()
    mine = owner_band == b

    @pl.when(mine)
    def _():
        sent = cells.at[0:56]
        pltpu.make_async_copy(sent, sent, send_sem.at[4]).wait()

    @pl.when(jnp.logical_not(mine))
    def _():
        pltpu.make_async_copy(cells, cells, send_sem.at[4]).wait()


def body(alm, legendre, order_of_slot):
    any_space = pl.BlockSpec(memory_space=pl.ANY)
    vmem = pl.BlockSpec(memory_space=pltpu.VMEM)
    first, twid, second, back, last = tables()
    return pl.pallas_call(
        kernel,
        out_shape=(
            jax.ShapeDtypeStruct((16, 512), F32),
            jax.ShapeDtypeStruct((16, 2, 128), F32),
        ),
        in_specs=[any_space] * 8,
        out_specs=(vmem, vmem),
        scratch_shapes=scratch_list()
        + [
            pltpu.SemaphoreType.DMA((11,)),
            pltpu.SemaphoreType.DMA((5,)),
            pltpu.SemaphoreType.DMA((5,)),
            pltpu.SemaphoreType.DMA((NT,)),
        ],
        compiler_params=pltpu.CompilerParams(
            collective_id=0, has_side_effects=True, vmem_limit_bytes=67043328
        ),
    )(alm, legendre, order_of_slot.reshape(8, 128), first, twid, second, back, last)


def solution(mesh):
    placed = (P("band", None, None, "tile"), P("band", "tile", None), P())
    return jax.shard_map(
        body,
        mesh=mesh,
        in_specs=placed,
        out_specs=(P("band", "tile"), P("band", None, "tile")),
        check_vma=False,
    )
```

```python
import math

import jax
import jax.numpy as jnp
import numpy as np
from jax import lax
from jax.experimental import pallas as pl
from jax.experimental.pallas import tpu as pltpu
from jax.sharding import PartitionSpec as P

C = 9
HALO = 32
RIDGE = 0.1
EPSILON = 1e-06
NB = 64
NT = 8
F32 = jnp.float32
BF16 = jnp.bfloat16
MESH = pl.DeviceIdType.MESH


SCRATCH = {
    "alm_v": ((16, C, 2, 128), BF16),
    "leg_v": ((16, 128, 1024), BF16),
    "ord_v": ((8, 128), jnp.int32),
    "narrow": ((768, 128), BF16),
    "twid": ((128, 128), F32),
    "stage": ((NT, 288, 128), F32),
    "parts": ((NT, 288, 128), BF16),
    "heard": ((NT, 288, 128), BF16),
    "slot_s": ((NB, 3, 2, 128), BF16),
    "slot_r": ((NB, 3, 2, 128), BF16),
    "turned": ((384, 128), F32),
    "modes": ((8, 48, 128), F32),
    "gathered": ((C, 32, 128), F32),
    "to_order": ((1024, 1024), BF16),
    "to_slot": ((1024, 1024), BF16),
    "maps": ((C, 64, 128), F32),
    "smoothed": ((45, 64, 128), F32),
    "ilc": ((64, 128), F32),
    "cells": ((64, 128), F32),
    "cells_r": ((64, 128), F32),
    "spec": ((128, 128), F32),
    "spec_s": ((16, 2, 128), BF16),
    "spec_r": ((NB, 2, 128), BF16),
    "spec_t": ((128, 128), F32),
    "every": ((NT, 32, 128), BF16),
    "sums": ((16, 32, 128), F32),
}


def scratch_list():
    return [pltpu.VMEM(shape, kind) for shape, kind in SCRATCH.values()]


def tables():
    xl, j, xs = np.meshgrid(np.arange(8), np.arange(2), np.arange(4), indexing="ij")
    xa, jr = (xl + 8 * xs).reshape(-1), j.reshape(-1)
    m0, m1 = np.arange(128), np.arange(8)
    ang = 2 * np.pi * ((xa[:, None] * m1[None, :]) % 32) / 32
    same = (jr[:, None, None] == np.arange(2)[None, None, :]).astype(np.float64)
    cs, sn = np.cos(ang)[:, :, None] * same, np.sin(ang)[:, :, None] * same
    real = np.stack([cs, -sn], axis=3).reshape(64, 32)
    imag = np.stack([sn, cs], axis=3).reshape(64, 32)
    first = np.concatenate([real, imag], axis=0)
    high = first.astype(BF16).astype(np.float64)
    first = np.concatenate([high, first - high], axis=1)
    ang = 2 * np.pi * (xa[:, None] * m0[None, :]) / 4096
    twiddle = np.stack([np.cos(ang), np.sin(ang)])
    ang = 2 * np.pi * ((m0[:, None] * m0[None, :]) % 128) / 128
    second = np.concatenate([np.cos(ang), -np.sin(ang)], axis=0) / 32
    back = np.concatenate([np.cos(ang), -np.sin(ang)], axis=1) / 32
    ang = 2 * np.pi * ((m1[:, None] * xa[None, :]) % 32) / 32
    same = (np.arange(2)[:, None, None] == jr[None, None, :]).astype(np.float64)
    cs, sn = np.cos(ang)[None] * same, np.sin(ang)[None] * same
    e0 = np.concatenate([cs, sn], axis=2).reshape(16, 128)
    e1 = np.concatenate([-sn, cs], axis=2).reshape(16, 128)
    none = np.zeros((48, 128))
    last = np.concatenate([e0, none, e1, none], axis=0)
    first = np.concatenate([first, np.zeros((128, 64))], axis=1)
    narrow = [first, second, back[:, :128], back[:, 128:], last]
    twiddle = np.concatenate([twiddle.reshape(128, 128), np.zeros((384, 128))], axis=0)
    return np.concatenate(narrow, axis=0).astype(BF16), twiddle.astype(np.float32)


def pair_table():
    return [(a, b) for a in range(C) for b in range(a, C)]


def window_sums(maps, smoothed):
    sub = lax.broadcasted_iota(jnp.int32, (8, 128), 0) % 4
    below = [jnp.where(sub >= k, 1.0, 0.0).astype(F32) for k in (1, 2, 3)]
    above = [jnp.where(sub <= 3 - k, 1.0, 0.0).astype(F32) for k in (1, 2, 3)]
    for at, (a, b) in enumerate(pair_table()):
        prod = [
            maps[a, 8 * i : 8 * i + 8, :] * maps[b, 8 * i : 8 * i + 8, :] for i in range(8)
        ]
        pre, post = [prod[0]], [prod[7]]
        for i in range(1, 8):
            pre.append(pre[-1] + prod[i])
            post.append(post[-1] + prod[7 - i])
        post = post[::-1]
        seg = pre[7]
        low = high = None
        for k in (1, 2, 3):
            down = below[k - 1] * pltpu.roll(seg, k, 0)
            up = above[k - 1] * pltpu.roll(seg, 8 - k, 0)
            low = down if low is None else low + down
            high = up if high is None else high + up
        total = seg + low + high
        for i in range(8):
            before = pltpu.roll(post[i] + high, 1, 1)
            after = pltpu.roll(pre[i] + low, 127, 1)
            smoothed[at, 8 * i : 8 * i + 8, :] = (before + total + after) * (
                1.0 / (2 * HALO + 1)
            )


def solve_cells(maps, smoothed, out):
    index = {}
    for at, (a, b) in enumerate(pair_table()):
        index[a, b] = at

    def step(i, _):
        rows = pl.ds(pl.multiple_of(i * 8, 8), 8)
        left = {key: smoothed[at, rows, :] for key, at in index.items()}
        trace = left[0, 0]
        for c in range(1, C):
            trace = trace + left[c, c]
        ridge = RIDGE * (trace * (1.0 / C) + EPSILON)
        for c in range(C):
            left[c, c] = left[c, c] + ridge
        ones = [jnp.ones((8, 128), F32) for _ in range(C)]
        vals = [maps[c, rows, :] for c in range(C)]
        top = bottom = None
        for k in range(C):
            inverse = 1.0 / left[k, k]
            scaled = ones[k] * inverse
            add_b, add_t = scaled * ones[k], scaled * vals[k]
            bottom = add_b if bottom is None else bottom + add_b
            top = add_t if top is None else top + add_t
            for r in range(k + 1, C):
                ratio = left[k, r] * inverse
                for q in range(r, C):
                    left[r, q] = left[r, q] - ratio * left[k, q]
                ones[r] = ones[r] - ratio * ones[k]
                vals[r] = vals[r] - ratio * vals[k]
        out[rows, :] = top / bottom
        return 0

    lax.fori_loop(0, 8, step, 0)


def band_peer(d, b):
    k, i = lax.div(d, 4), lax.rem(d, 4)
    dz = lax.rem(24 + (1 - 2 * lax.rem(k, 2)) * lax.div(k + 1, 2), 16)
    x = lax.rem(lax.div(b, 32) + lax.div(i, 2) + 1, 2)
    z = lax.rem(lax.rem(lax.div(b, 2), 16) + dz, 16)
    core = lax.rem(lax.rem(b, 2) + lax.rem(i, 2) + 1, 2)
    return (x * 16 + z) * 2 + core


def along_z(b, dz):
    z = lax.rem(lax.rem(lax.div(b, 2), 16) + dz, 16)
    return (lax.div(b, 32) * 16 + z) * 2 + lax.rem(b, 2)


def same_z(b, i):
    x = lax.rem(lax.div(b, 32) + i // 2, 2)
    return (x * 16 + lax.rem(lax.div(b, 2), 16)) * 2 + lax.rem(lax.rem(b, 2) + i % 2, 2)


FAR_FIRST = ((2, 1), (1, 1), (3, 1), (2, 0), (0, 1), (1, 0), (3, 0))


def tile_peer(t, dy, dx):
    return 2 * lax.rem(lax.div(t, 2) + dy, 4) + lax.rem(lax.rem(t, 2) + dx, 2)


def turn(block):
    return jnp.transpose(block, (1, 0))


def kernel(
    alm_h, leg_h, ord_h, narrow_h, twid_h,
    map_o, alm_o,
    alm_v, leg_v, ord_v, narrow, twid,
    stage, parts, heard, slot_s, slot_r, turned, modes, gathered, to_order, to_slot,
    maps, smoothed, ilc, cells, cells_r, spec, spec_s, spec_r, spec_t, every, sums,
    load_sem, send_sem, recv_sem, tile_sem, greet_sem,
):
    b = lax.axis_index("band")
    t = lax.axis_index("tile")
    owner_band = 8 * t + lax.div(b, 8)
    lane = lax.broadcasted_iota(jnp.int32, (8, 128), 1)

    loads = []
    for at, (src, dst) in enumerate(
        [(alm_h, alm_v)]
        + [(leg_h.at[pl.ds(4 * k, 4)], leg_v.at[pl.ds(4 * k, 4)]) for k in range(4)]
        + [(ord_h, ord_v), (narrow_h, narrow), (twid_h.at[pl.ds(0, 128)], twid)]
    ):
        copy = pltpu.make_async_copy(src, dst, load_sem.at[at])
        copy.start()
        loads.append(copy)

    bar = pltpu.get_barrier_semaphore()

    def greet(sem, others):
        for band, tile in others:
            pl.semaphore_signal(
                sem, inc=1, device_id={"band": band, "tile": tile}, device_id_type=MESH
            )

    greet(bar, [(b, tile_peer(t, dy, dx)) for dy, dx in FAR_FIRST])
    greet(bar, [(along_z(b, dz), t) for dz in (2, 14, 1, 15)])
    greet(bar, [(same_z(b, i), t) for i in (3, 2, 1)])

    loads[0].wait()
    for k in range(4):
        loads[1 + k].wait()
        for s in range(4 * k, 4 * k + 4):
            left = alm_v[s].reshape(18, 128)
            out = jnp.dot(left, leg_v[s], preferred_element_type=F32)
            for q in range(NT):
                stage[q, pl.ds(s, 18, stride=16), :] = out[:, 128 * q : 128 * q + 128]
    for q in range(NT):
        parts[q] = stage[q].astype(BF16)

    pl.semaphore_wait(bar, 14)
    greet(greet_sem.at[0], [(along_z(b, dz), t) for dz in (2, 14)])

    for dy, dx in FAR_FIRST:
        other = tile_peer(t, dy, dx)
        pltpu.make_async_remote_copy(
            src_ref=parts.at[other], dst_ref=heard.at[t], send_sem=send_sem.at[0],
            recv_sem=recv_sem.at[0], device_id={"band": b, "tile": other}, device_id_type=MESH,
        ).start()
    pltpu.make_async_copy(parts.at[t], heard.at[t], recv_sem.at[0]).start()

    for copy in loads[5:]:
        copy.wait()
    orders = ord_v[...].astype(F32)
    cols = turn(jnp.concatenate([orders, jnp.zeros((120, 128), F32)], axis=0))
    turned[0:128, :] = cols
    wide = lax.broadcasted_iota(jnp.int32, (8, 1024), 1).astype(F32)
    for s in range(16):
        pick = turned[pl.ds(s, 8, stride=16), :]
        for h in range(0, 8, 2):
            rows = [
                jnp.where(pick[:, k : k + 1] == wide, 1.0, 0.0) for k in (h, h + 1)
            ]
            to_order[s * 64 + h * 8 : s * 64 + h * 8 + 16, :] = jnp.concatenate(
                rows, axis=0
            ).astype(BF16)
    pl.semaphore_wait(greet_sem.at[0], 2)
    greet(greet_sem.at[1], [(along_z(b, dz), t) for dz in (4, 12)])
    orders = ord_v[...].astype(F32)
    tall = lax.broadcasted_iota(jnp.int32, (128, 128), 0).astype(F32)
    for h in range(8):
        row = jnp.broadcast_to(orders[h : h + 1, :], (128, 128))
        for k in range(8):
            to_slot[128 * k : 128 * k + 128, 128 * h : 128 * h + 128] = jnp.where(
                row == tall + 128.0 * k, 1.0, 0.0
            ).astype(BF16)

    pl.semaphore_wait(greet_sem.at[1], 2)
    greet(greet_sem.at[2], [(same_z(b, i), t) for i in (3, 2, 1)])
    pltpu.make_async_copy(heard, heard, recv_sem.at[0]).wait()
    total = heard[0].astype(F32)
    for q in range(1, NT):
        total = total + heard[q].astype(F32)
    total = jnp.concatenate([total, jnp.zeros((96, 128), F32)], axis=0)
    for k in range(3):
        block = turn(total[128 * k : 128 * k + 128])
        slot_s[:, k] = block.astype(BF16).reshape(NB, 2, 128)

    def send_slots(d, _):
        other = band_peer(d, b)
        pltpu.make_async_remote_copy(
            src_ref=slot_s.at[other], dst_ref=slot_r.at[b], send_sem=send_sem.at[1],
            recv_sem=recv_sem.at[1], device_id={"band": other, "tile": t}, device_id_type=MESH,
        ).start()
        return 0

    pl.semaphore_wait(greet_sem.at[2], 3)
    lax.fori_loop(0, NB - 1, send_slots, 0)
    pltpu.make_async_copy(slot_s.at[b], slot_r.at[b], recv_sem.at[1]).start()
    pltpu.make_async_copy(slot_r, slot_r, recv_sem.at[1]).wait()

    for k in range(3):
        block = slot_r[:, k].astype(F32)
        block = jnp.concatenate([block[:, 0, :], block[:, 1, :]], axis=0)
        turned[128 * k : 128 * k + 128, :] = turn(block)
    lane24 = lax.broadcasted_iota(jnp.int32, (24, 128), 1)
    pieces = []
    for p in range(8):
        even = turned[pl.ds(2 * p, 24, stride=16), :]
        odd = turned[pl.ds(2 * p + 1, 24, stride=16), :]
        first_r = jnp.where(lane24 < 64, even, pltpu.roll(odd, 64, 1))
        second_r = jnp.where(lane24 < 64, pltpu.roll(even, 64, 1), odd)
        pieces.append(jnp.concatenate([first_r, second_r], axis=0).astype(BF16))
    ordered = jnp.dot(
        jnp.concatenate(pieces, axis=1), to_order[...], preferred_element_type=F32
    )
    for k in range(8):
        modes[k] = ordered[:, 128 * k : 128 * k + 128]
    for c in range(C):
        for k in range(8):
            gathered[c, 4 * k : 4 * k + 2, :] = modes[k, 2 * c : 2 * c + 2, :]
            gathered[c, 4 * k + 2 : 4 * k + 4, :] = modes[k, 24 + 2 * c : 26 + 2 * c, :]

    twr, twi = twid[0:64, :], twid[64:128, :]
    for c in range(C):
        data = gathered[c].astype(BF16)
        grid = jnp.dot(
            narrow[0:128, 0:64], jnp.concatenate([data, data], axis=0), preferred_element_type=F32
        )
        re, im = grid[:64], grid[64:]
        both = jnp.concatenate([re * twr - im * twi, re * twi + im * twr], axis=1)
        maps[c] = (
            jnp.dot(both.astype(BF16), narrow[128:384, :], preferred_element_type=F32)
            .astype(BF16)
            .astype(F32)
        )

    window_sums(maps, smoothed)
    solve_cells(maps, smoothed, ilc)

    twr, twi = twid[0:64, :], twid[64:128, :]
    low = ilc[...].astype(BF16)
    re = jnp.dot(low, narrow[384:512, :], preferred_element_type=F32)
    im = jnp.dot(low, narrow[512:640, :], preferred_element_type=F32)
    both = jnp.concatenate([re * twr + im * twi, im * twr - re * twi], axis=0)
    spec[...] = jnp.dot(narrow[640:768, :], both.astype(BF16), preferred_element_type=F32)
    flat = jnp.concatenate([spec[pl.ds(k, 16, stride=8), :] for k in range(8)], axis=1)
    placed = jnp.dot(flat.astype(BF16), to_slot[...], preferred_element_type=F32)
    half = lax.broadcasted_iota(jnp.int32, (8, 128), 1) < 64
    for k in range(8):
        e0, e1 = (placed[8 * e : 8 * e + 8, 128 * k : 128 * k + 128] for e in range(2))
        low = jnp.where(half, e0, pltpu.roll(e1, 64, 1))
        high = jnp.where(half, pltpu.roll(e0, 64, 1), e1)
        spec_s[2 * k] = low[0:2].astype(BF16)
        spec_s[2 * k + 1] = high[0:2].astype(BF16)
    def send_spectra(d, _):
        other = band_peer(d, b)
        pltpu.make_async_remote_copy(
            src_ref=spec_s.at[lax.div(other, 4)], dst_ref=spec_r.at[b], send_sem=send_sem.at[2],
            recv_sem=recv_sem.at[2], device_id={"band": other, "tile": t}, device_id_type=MESH,
        ).start()
        return 0

    lax.fori_loop(0, NB - 1, send_spectra, 0)
    pltpu.make_async_copy(spec_s.at[lax.div(b, 4)], spec_r.at[b], recv_sem.at[2]).start()

    lines = jnp.concatenate(
        [ilc[pl.ds(k, 8, stride=8), :] for k in range(8)] + [jnp.zeros((64, 128), F32)], axis=0
    )
    turned[0:128, :] = turn(lines)
    lane32 = lax.broadcasted_iota(jnp.int32, (32, 128), 1)
    for j in range(2):
        line = None
        for k in range(4):
            part = turned[pl.ds(k, 32, stride=4), :]
            part = pltpu.roll(part, (32 * k - 32 * j) % 128, 1) if k != j else part
            keep = jnp.logical_and(lane32 >= 32 * k, lane32 < 32 * k + 32)
            part = jnp.where(keep, part, 0.0)
            line = part if line is None else line + part
        cells[pl.ds(j, 32, stride=2), :] = line
    place = pl.ds(pl.multiple_of(8 * lax.rem(b, 8), 8), 8)
    for q in range(NT):
        own = jnp.logical_and(owner_band == b, t == q)

        @pl.when(own)
        def _():
            pltpu.make_async_copy(
                cells.at[8 * q : 8 * q + 8], cells_r.at[place], recv_sem.at[4]
            ).start()

        @pl.when(jnp.logical_not(own))
        def _():
            pltpu.make_async_remote_copy(
                src_ref=cells.at[8 * q : 8 * q + 8], dst_ref=cells_r.at[place],
                send_sem=send_sem.at[4], recv_sem=recv_sem.at[4],
                device_id={"band": owner_band, "tile": q}, device_id_type=MESH,
            ).start()

    pltpu.make_async_copy(spec_r, spec_r, recv_sem.at[2]).wait()
    spec_t[...] = turn(spec_r[...].astype(F32).reshape(128, 128))
    start = 16 * lax.rem(b, 4)
    own_s = [spec_t[pl.ds(pl.multiple_of(64 * e + start, 16), 16), :] for e in range(2)]
    every[t] = jnp.concatenate(own_s, axis=0).astype(BF16)
    for dy, dx in FAR_FIRST:
        other = tile_peer(t, dy, dx)
        pltpu.make_async_remote_copy(
            src_ref=every.at[t], dst_ref=every.at[t], send_sem=send_sem.at[3],
            recv_sem=tile_sem.at[t], device_id={"band": b, "tile": other}, device_id_type=MESH,
        ).start()
    for at, (dy, dx) in enumerate(((0, 0),) + FAR_FIRST[::-1]):
        other = tile_peer(t, dy, dx)
        if at:
            pltpu.make_async_copy(every.at[other], every.at[other], tile_sem.at[other]).wait()
        block = every[other]
        cycles = pl.ds(pl.multiple_of(128 * other, 128), 128)
        for s in range(16):
            out = lax.dot_general(
                block, leg_v[s, :, cycles], (((1,), (1,)), ((), ())), preferred_element_type=F32
            )
            if at == 0:
                sums[s] = out
            elif at < NT - 1:
                sums[s] += out
            else:
                out = out + sums[s]
                alm_o[s, 0:1, :] = out[s : s + 1]
                alm_o[s, 1:2, :] = out[16 + s : 17 + s]

    pltpu.make_async_copy(cells_r, cells_r, recv_sem.at[4]).wait()
    for q in range(4):
        for j in range(2):
            ilc[pl.ds(16 * q + j, 8, stride=2), :] = cells_r[pl.ds(2 * q + j, 8, stride=8), :]
        map_o[:, 128 * q : 128 * q + 128] = ilc[16 * q : 16 * q + 16, :]

    sent = parts.at[pl.ds(0, NT - 1)]
    pltpu.make_async_copy(sent, sent, send_sem.at[0]).wait()
    sent = slot_s.at[pl.ds(0, NB - 1)]
    pltpu.make_async_copy(sent, sent, send_sem.at[1]).wait()
    sent = spec_r.at[pl.ds(0, NB - 1)]
    pltpu.make_async_copy(sent, sent, send_sem.at[2]).wait()
    sent = every.at[pl.ds(0, NT - 1)]
    pltpu.make_async_copy(sent, sent, send_sem.at[3]).wait()
    mine = owner_band == b

    @pl.when(mine)
    def _():
        sent = cells.at[0:56]
        pltpu.make_async_copy(sent, sent, send_sem.at[4]).wait()

    @pl.when(jnp.logical_not(mine))
    def _():
        pltpu.make_async_copy(cells, cells, send_sem.at[4]).wait()


def body(alm, legendre, order_of_slot):
    hbm = pl.BlockSpec(memory_space=pltpu.HBM)
    vmem = pl.BlockSpec(memory_space=pltpu.VMEM)
    narrow, twid = tables()
    operands = (alm, legendre, order_of_slot.reshape(8, 128), jnp.asarray(narrow), jnp.asarray(twid))
    operands = [pltpu.with_memory_space_constraint(x, pltpu.HBM) for x in operands]
    return pl.pallas_call(
        kernel,
        out_shape=(
            jax.ShapeDtypeStruct((16, 512), F32),
            jax.ShapeDtypeStruct((16, 2, 128), F32),
        ),
        in_specs=[hbm] * 5,
        out_specs=(vmem, vmem),
        scratch_shapes=scratch_list()
        + [
            pltpu.SemaphoreType.DMA((8,)),
            pltpu.SemaphoreType.DMA((5,)),
            pltpu.SemaphoreType.DMA((5,)),
            pltpu.SemaphoreType.DMA((NT,)),
            pltpu.SemaphoreType.REGULAR((3,)),
        ],
        compiler_params=pltpu.CompilerParams(
            collective_id=0, has_side_effects=True, vmem_limit_bytes=48 * 1024 * 1024
        ),
    )(*operands)


def solution(mesh):
    placed = (P("band", None, None, "tile"), P("band", "tile", None), P())
    return jax.shard_map(
        body,
        mesh=mesh,
        in_specs=placed,
        out_specs=(P("band", "tile"), P("band", None, "tile")),
        check_vma=False,
    )
```

```python
import math

import jax
import jax.numpy as jnp
import numpy as np
from jax import lax
from jax.experimental import pallas as pl
from jax.experimental.pallas import tpu as pltpu
from jax.sharding import PartitionSpec as P

C = 9
HALO = 32
RIDGE = 0.1
EPSILON = 1e-06
NB = 64
NT = 8
F32 = jnp.float32
BF16 = jnp.bfloat16
MESH = pl.DeviceIdType.MESH


SCRATCH = {
    "alm_v": ((16, C, 2, 128), BF16),
    "leg_v": ((16, 128, 1024), BF16),
    "ord_v": ((8, 128), jnp.int32),
    "narrow": ((768, 128), BF16),
    "twid": ((128, 128), F32),
    "stage": ((NT, 288, 128), F32),
    "parts": ((NT, 288, 128), BF16),
    "heard": ((NT, 288, 128), BF16),
    "slot_s": ((NB, 3, 2, 128), BF16),
    "slot_r": ((NB, 3, 2, 128), BF16),
    "turned": ((384, 128), F32),
    "modes": ((8, 48, 128), F32),
    "gathered": ((C, 32, 128), F32),
    "to_order": ((1024, 1024), BF16),
    "to_slot": ((1024, 1024), BF16),
    "maps": ((C, 64, 128), F32),
    "ahead": ((C, 64, 128), F32),
    "smoothed": ((45, 64, 128), F32),
    "ilc": ((64, 128), F32),
    "cells": ((64, 128), F32),
    "cells_r": ((64, 128), F32),
    "spec": ((128, 128), F32),
    "spec_s": ((16, 2, 128), BF16),
    "spec_r": ((NB, 2, 128), BF16),
    "spec_t": ((128, 128), F32),
    "every": ((NT, 32, 128), BF16),
    "sums": ((16, 32, 128), F32),
}


def scratch_list():
    return [pltpu.VMEM(shape, kind) for shape, kind in SCRATCH.values()]


def tables():
    xl, j, xs = np.meshgrid(np.arange(8), np.arange(2), np.arange(4), indexing="ij")
    xa, jr = (xl + 8 * xs).reshape(-1), j.reshape(-1)
    m0, m1 = np.arange(128), np.arange(8)
    ang = 2 * np.pi * ((xa[:, None] * m1[None, :]) % 32) / 32
    same = (jr[:, None, None] == np.arange(2)[None, None, :]).astype(np.float64)
    cs, sn = np.cos(ang)[:, :, None] * same, np.sin(ang)[:, :, None] * same
    real = np.stack([cs, -sn], axis=3).reshape(64, 32)
    imag = np.stack([sn, cs], axis=3).reshape(64, 32)
    first = np.concatenate([real, imag], axis=0)
    high = first.astype(BF16).astype(np.float64)
    first = np.concatenate([high, first - high], axis=1)
    ang = 2 * np.pi * (xa[:, None] * m0[None, :]) / 4096
    twiddle = np.stack([np.cos(ang), np.sin(ang)])
    ang = 2 * np.pi * ((m0[:, None] * m0[None, :]) % 128) / 128
    second = np.concatenate([np.cos(ang), -np.sin(ang)], axis=0) / 32
    back = np.concatenate([np.cos(ang), -np.sin(ang)], axis=1) / 32
    ang = 2 * np.pi * ((m1[:, None] * xa[None, :]) % 32) / 32
    same = (np.arange(2)[:, None, None] == jr[None, None, :]).astype(np.float64)
    cs, sn = np.cos(ang)[None] * same, np.sin(ang)[None] * same
    e0 = np.concatenate([cs, sn], axis=2).reshape(16, 128)
    e1 = np.concatenate([-sn, cs], axis=2).reshape(16, 128)
    none = np.zeros((48, 128))
    last = np.concatenate([e0, none, e1, none], axis=0)
    first = np.concatenate([first, np.zeros((128, 64))], axis=1)
    narrow = [first, second, back[:, :128], back[:, 128:], last]
    twiddle = np.concatenate([twiddle.reshape(128, 128), np.zeros((384, 128))], axis=0)
    return np.concatenate(narrow, axis=0).astype(BF16), twiddle.astype(np.float32)


def pair_table():
    return [(a, b) for a in range(C) for b in range(a, C)]


def window_sums(maps, smoothed):
    sub = lax.broadcasted_iota(jnp.int32, (8, 128), 0) % 4
    below = [jnp.where(sub >= k, 1.0, 0.0).astype(F32) for k in (1, 2, 3)]
    above = [jnp.where(sub <= 3 - k, 1.0, 0.0).astype(F32) for k in (1, 2, 3)]
    for at, (a, b) in enumerate(pair_table()):
        prod = [
            maps[a, 8 * i : 8 * i + 8, :] * maps[b, 8 * i : 8 * i + 8, :] for i in range(8)
        ]
        pre, post = [prod[0]], [prod[7]]
        for i in range(1, 8):
            pre.append(pre[-1] + prod[i])
            post.append(post[-1] + prod[7 - i])
        post = post[::-1]
        seg = pre[7]
        low = high = None
        for k in (1, 2, 3):
            down = below[k - 1] * pltpu.roll(seg, k, 0)
            up = above[k - 1] * pltpu.roll(seg, 8 - k, 0)
            low = down if low is None else low + down
            high = up if high is None else high + up
        base = high + pltpu.roll(seg + low + high, 127, 1) + pltpu.roll(low, 126, 1)
        for i in range(8):
            smoothed[at, 8 * i : 8 * i + 8, :] = post[i] + base + pltpu.roll(pre[i], 126, 1)


def solve_cells(ahead, smoothed, out):
    index = {}
    for at, (a, b) in enumerate(pair_table()):
        index[a, b] = at

    def step(i, _):
        rows = pl.ds(pl.multiple_of(i * 8, 8), 8)
        left = {key: smoothed[at, rows, :] for key, at in index.items()}
        trace = left[0, 0]
        for c in range(1, C):
            trace = trace + left[c, c]
        ridge = RIDGE * (trace * (1.0 / C) + EPSILON * (2 * HALO + 1))
        for c in range(C):
            left[c, c] = left[c, c] + ridge
        ones = [jnp.ones((8, 128), F32) for _ in range(C)]
        vals = [ahead[c, rows, :] for c in range(C)]
        top = bottom = None
        for k in range(C):
            inverse = 1.0 / left[k, k]
            scaled = ones[k] * inverse
            add_b, add_t = scaled * ones[k], scaled * vals[k]
            bottom = add_b if bottom is None else bottom + add_b
            top = add_t if top is None else top + add_t
            for r in range(k + 1, C):
                ratio = left[k, r] * inverse
                for q in range(r, C):
                    left[r, q] = left[r, q] - ratio * left[k, q]
                ones[r] = ones[r] - ratio * ones[k]
                vals[r] = vals[r] - ratio * vals[k]
        out[rows, :] = top / bottom
        return 0

    lax.fori_loop(0, 8, step, 0, unroll=8)


def band_peer(d, b):
    k, i = lax.div(d, 4), lax.rem(d, 4)
    dz = lax.rem(24 + (1 - 2 * lax.rem(k, 2)) * lax.div(k + 1, 2), 16)
    x = lax.rem(lax.div(b, 32) + lax.div(i, 2) + 1, 2)
    z = lax.rem(lax.rem(lax.div(b, 2), 16) + dz, 16)
    core = lax.rem(lax.rem(b, 2) + lax.rem(i, 2) + 1, 2)
    return (x * 16 + z) * 2 + core


def along_z(b, dz):
    z = lax.rem(lax.rem(lax.div(b, 2), 16) + dz, 16)
    return (lax.div(b, 32) * 16 + z) * 2 + lax.rem(b, 2)


def same_z(b, i):
    x = lax.rem(lax.div(b, 32) + i // 2, 2)
    return (x * 16 + lax.rem(lax.div(b, 2), 16)) * 2 + lax.rem(lax.rem(b, 2) + i % 2, 2)


FAR_FIRST = ((2, 1), (1, 1), (3, 1), (2, 0), (0, 1), (1, 0), (3, 0))


def tile_peer(t, dy, dx):
    return 2 * lax.rem(lax.div(t, 2) + dy, 4) + lax.rem(lax.rem(t, 2) + dx, 2)


def turn(block):
    return jnp.transpose(block, (1, 0))


def kernel(
    alm_h, leg_h, ord_h, narrow_h, twid_h,
    map_o, alm_o,
    alm_v, leg_v, ord_v, narrow, twid,
    stage, parts, heard, slot_s, slot_r, turned, modes, gathered, to_order, to_slot,
    maps, ahead, smoothed, ilc, cells, cells_r, spec, spec_s, spec_r, spec_t, every, sums,
    load_sem, send_sem, recv_sem, tile_sem, greet_sem,
):
    b = lax.axis_index("band")
    t = lax.axis_index("tile")
    owner_band = 8 * t + lax.div(b, 8)
    lane = lax.broadcasted_iota(jnp.int32, (8, 128), 1)

    loads = []
    for at, (src, dst) in enumerate(
        [(alm_h, alm_v)]
        + [(leg_h.at[pl.ds(4 * k, 4)], leg_v.at[pl.ds(4 * k, 4)]) for k in range(4)]
        + [(ord_h, ord_v), (narrow_h, narrow), (twid_h.at[pl.ds(0, 128)], twid)]
    ):
        copy = pltpu.make_async_copy(src, dst, load_sem.at[at])
        copy.start()
        loads.append(copy)

    bar = pltpu.get_barrier_semaphore()

    def greet(sem, others):
        for band, tile in others:
            pl.semaphore_signal(
                sem, inc=1, device_id={"band": band, "tile": tile}, device_id_type=MESH
            )

    greet(bar, [(b, tile_peer(t, dy, dx)) for dy, dx in FAR_FIRST])
    greet(bar, [(along_z(b, dz), t) for dz in (2, 14, 1, 15)])
    greet(bar, [(same_z(b, i), t) for i in (3, 2, 1)])

    loads[0].wait()
    for k in range(4):
        loads[1 + k].wait()
        for s in range(4 * k, 4 * k + 4):
            left = alm_v[s].reshape(18, 128)
            out = jnp.dot(left, leg_v[s], preferred_element_type=F32)
            for q in range(NT):
                stage[q, pl.ds(s, 18, stride=16), :] = out[:, 128 * q : 128 * q + 128]
    for q in range(NT):
        parts[q] = stage[q].astype(BF16)

    pl.semaphore_wait(bar, 14)
    greet(greet_sem.at[0], [(along_z(b, dz), t) for dz in (2, 14)])

    for dy, dx in FAR_FIRST:
        other = tile_peer(t, dy, dx)
        pltpu.make_async_remote_copy(
            src_ref=parts.at[other], dst_ref=heard.at[t], send_sem=send_sem.at[0],
            recv_sem=recv_sem.at[0], device_id={"band": b, "tile": other}, device_id_type=MESH,
        ).start()
    pltpu.make_async_copy(parts.at[t], heard.at[t], recv_sem.at[0]).start()

    for copy in loads[5:]:
        copy.wait()
    orders = ord_v[...].astype(F32)
    cols = turn(jnp.concatenate([orders, jnp.zeros((120, 128), F32)], axis=0))
    turned[0:128, :] = cols
    wide = lax.broadcasted_iota(jnp.int32, (8, 1024), 1).astype(F32)
    for s in range(16):
        pick = turned[pl.ds(s, 8, stride=16), :]
        for h in range(0, 8, 2):
            rows = [
                jnp.where(pick[:, k : k + 1] == wide, 1.0, 0.0) for k in (h, h + 1)
            ]
            to_order[s * 64 + h * 8 : s * 64 + h * 8 + 16, :] = jnp.concatenate(
                rows, axis=0
            ).astype(BF16)
    pl.semaphore_wait(greet_sem.at[0], 2)
    greet(greet_sem.at[1], [(along_z(b, dz), t) for dz in (4, 12)])
    orders = ord_v[...].astype(F32)
    tall = lax.broadcasted_iota(jnp.int32, (128, 128), 0).astype(F32)
    for h in range(8):
        row = jnp.broadcast_to(orders[h : h + 1, :], (128, 128))
        for k in range(8):
            to_slot[128 * k : 128 * k + 128, 128 * h : 128 * h + 128] = jnp.where(
                row == tall + 128.0 * k, 1.0, 0.0
            ).astype(BF16)

    pl.semaphore_wait(greet_sem.at[1], 2)
    greet(greet_sem.at[2], [(same_z(b, i), t) for i in (3, 2, 1)])
    pltpu.make_async_copy(heard, heard, recv_sem.at[0]).wait()
    total = heard[0].astype(F32)
    for q in range(1, NT):
        total = total + heard[q].astype(F32)
    total = jnp.concatenate([total, jnp.zeros((96, 128), F32)], axis=0)
    for k in range(3):
        block = turn(total[128 * k : 128 * k + 128])
        slot_s[:, k] = block.astype(BF16).reshape(NB, 2, 128)

    def send_slots(d, _):
        other = band_peer(d, b)
        pltpu.make_async_remote_copy(
            src_ref=slot_s.at[other], dst_ref=slot_r.at[b], send_sem=send_sem.at[1],
            recv_sem=recv_sem.at[1], device_id={"band": other, "tile": t}, device_id_type=MESH,
        ).start()
        return 0

    pl.semaphore_wait(greet_sem.at[2], 3)
    lax.fori_loop(0, NB - 1, send_slots, 0)
    pltpu.make_async_copy(slot_s.at[b], slot_r.at[b], recv_sem.at[1]).start()
    pltpu.make_async_copy(slot_r, slot_r, recv_sem.at[1]).wait()

    for k in range(3):
        block = slot_r[:, k].astype(F32)
        block = jnp.concatenate([block[:, 0, :], block[:, 1, :]], axis=0)
        turned[128 * k : 128 * k + 128, :] = turn(block)
    lane24 = lax.broadcasted_iota(jnp.int32, (24, 128), 1)
    pieces = []
    for p in range(8):
        even = turned[pl.ds(2 * p, 24, stride=16), :]
        odd = turned[pl.ds(2 * p + 1, 24, stride=16), :]
        first_r = jnp.where(lane24 < 64, even, pltpu.roll(odd, 64, 1))
        second_r = jnp.where(lane24 < 64, pltpu.roll(even, 64, 1), odd)
        pieces.append(jnp.concatenate([first_r, second_r], axis=0).astype(BF16))
    ordered = jnp.dot(
        jnp.concatenate(pieces, axis=1), to_order[...], preferred_element_type=F32
    )
    for k in range(8):
        modes[k] = ordered[:, 128 * k : 128 * k + 128]
    for c in range(C):
        for k in range(8):
            gathered[c, 4 * k : 4 * k + 2, :] = modes[k, 2 * c : 2 * c + 2, :]
            gathered[c, 4 * k + 2 : 4 * k + 4, :] = modes[k, 24 + 2 * c : 26 + 2 * c, :]

    twr, twi = twid[0:64, :], twid[64:128, :]
    for c in range(C):
        data = gathered[c].astype(BF16)
        grid = jnp.dot(
            narrow[0:128, 0:64], jnp.concatenate([data, data], axis=0), preferred_element_type=F32
        )
        re, im = grid[:64], grid[64:]
        both = jnp.concatenate([re * twr - im * twi, re * twi + im * twr], axis=1)
        found = jnp.dot(both.astype(BF16), narrow[128:384, :], preferred_element_type=F32)
        found = found.astype(BF16).astype(F32)
        maps[c] = found
        ahead[c] = pltpu.roll(found, 127, 1)

    window_sums(maps, smoothed)
    solve_cells(ahead, smoothed, ilc)
    ilc[...] = pltpu.roll(ilc[...], 1, 1)

    twr, twi = twid[0:64, :], twid[64:128, :]
    low = ilc[...].astype(BF16)
    re = jnp.dot(low, narrow[384:512, :], preferred_element_type=F32)
    im = jnp.dot(low, narrow[512:640, :], preferred_element_type=F32)
    both = jnp.concatenate([re * twr + im * twi, im * twr - re * twi], axis=0)
    spec[...] = jnp.dot(narrow[640:768, :], both.astype(BF16), preferred_element_type=F32)
    flat = jnp.concatenate([spec[pl.ds(k, 16, stride=8), :] for k in range(8)], axis=1)
    placed = jnp.dot(flat.astype(BF16), to_slot[...], preferred_element_type=F32)
    half = lax.broadcasted_iota(jnp.int32, (8, 128), 1) < 64
    for k in range(8):
        e0, e1 = (placed[8 * e : 8 * e + 8, 128 * k : 128 * k + 128] for e in range(2))
        low = jnp.where(half, e0, pltpu.roll(e1, 64, 1))
        high = jnp.where(half, pltpu.roll(e0, 64, 1), e1)
        spec_s[2 * k] = low[0:2].astype(BF16)
        spec_s[2 * k + 1] = high[0:2].astype(BF16)
    def send_spectra(d, _):
        other = band_peer(d, b)
        pltpu.make_async_remote_copy(
            src_ref=spec_s.at[lax.div(other, 4)], dst_ref=spec_r.at[b], send_sem=send_sem.at[2],
            recv_sem=recv_sem.at[2], device_id={"band": other, "tile": t}, device_id_type=MESH,
        ).start()
        return 0

    lax.fori_loop(0, NB - 1, send_spectra, 0)
    pltpu.make_async_copy(spec_s.at[lax.div(b, 4)], spec_r.at[b], recv_sem.at[2]).start()

    lines = jnp.concatenate(
        [ilc[pl.ds(k, 8, stride=8), :] for k in range(8)] + [jnp.zeros((64, 128), F32)], axis=0
    )
    turned[0:128, :] = turn(lines)
    lane32 = lax.broadcasted_iota(jnp.int32, (32, 128), 1)
    for j in range(2):
        line = None
        for k in range(4):
            part = turned[pl.ds(k, 32, stride=4), :]
            part = pltpu.roll(part, (32 * k - 32 * j) % 128, 1) if k != j else part
            keep = jnp.logical_and(lane32 >= 32 * k, lane32 < 32 * k + 32)
            part = jnp.where(keep, part, 0.0)
            line = part if line is None else line + part
        cells[pl.ds(j, 32, stride=2), :] = line
    place = pl.ds(pl.multiple_of(8 * lax.rem(b, 8), 8), 8)
    for q in range(NT):
        own = jnp.logical_and(owner_band == b, t == q)

        @pl.when(own)
        def _():
            pltpu.make_async_copy(
                cells.at[8 * q : 8 * q + 8], cells_r.at[place], recv_sem.at[4]
            ).start()

        @pl.when(jnp.logical_not(own))
        def _():
            pltpu.make_async_remote_copy(
                src_ref=cells.at[8 * q : 8 * q + 8], dst_ref=cells_r.at[place],
                send_sem=send_sem.at[4], recv_sem=recv_sem.at[4],
                device_id={"band": owner_band, "tile": q}, device_id_type=MESH,
            ).start()

    pltpu.make_async_copy(spec_r, spec_r, recv_sem.at[2]).wait()
    spec_t[...] = turn(spec_r[...].astype(F32).reshape(128, 128))
    start = 16 * lax.rem(b, 4)
    own_s = [spec_t[pl.ds(pl.multiple_of(64 * e + start, 16), 16), :] for e in range(2)]
    every[t] = jnp.concatenate(own_s, axis=0).astype(BF16)
    for dy, dx in FAR_FIRST:
        other = tile_peer(t, dy, dx)
        pltpu.make_async_remote_copy(
            src_ref=every.at[t], dst_ref=every.at[t], send_sem=send_sem.at[3],
            recv_sem=tile_sem.at[t], device_id={"band": b, "tile": other}, device_id_type=MESH,
        ).start()
    for at, (dy, dx) in enumerate(((0, 0),) + FAR_FIRST[::-1]):
        other = tile_peer(t, dy, dx)
        if at:
            pltpu.make_async_copy(every.at[other], every.at[other], tile_sem.at[other]).wait()
        block = every[other]
        cycles = pl.ds(pl.multiple_of(128 * other, 128), 128)
        for s in range(16):
            out = lax.dot_general(
                block, leg_v[s, :, cycles], (((1,), (1,)), ((), ())), preferred_element_type=F32
            )
            if at == 0:
                sums[s] = out
            elif at < NT - 1:
                sums[s] += out
            else:
                out = out + sums[s]
                alm_o[s, 0:1, :] = out[s : s + 1]
                alm_o[s, 1:2, :] = out[16 + s : 17 + s]

    pltpu.make_async_copy(cells_r, cells_r, recv_sem.at[4]).wait()
    for q in range(4):
        for j in range(2):
            ilc[pl.ds(16 * q + j, 8, stride=2), :] = cells_r[pl.ds(2 * q + j, 8, stride=8), :]
        map_o[:, 128 * q : 128 * q + 128] = ilc[16 * q : 16 * q + 16, :]

    sent = parts.at[pl.ds(0, NT - 1)]
    pltpu.make_async_copy(sent, sent, send_sem.at[0]).wait()
    sent = slot_s.at[pl.ds(0, NB - 1)]
    pltpu.make_async_copy(sent, sent, send_sem.at[1]).wait()
    sent = spec_r.at[pl.ds(0, NB - 1)]
    pltpu.make_async_copy(sent, sent, send_sem.at[2]).wait()
    sent = every.at[pl.ds(0, NT - 1)]
    pltpu.make_async_copy(sent, sent, send_sem.at[3]).wait()
    mine = owner_band == b

    @pl.when(mine)
    def _():
        sent = cells.at[0:56]
        pltpu.make_async_copy(sent, sent, send_sem.at[4]).wait()

    @pl.when(jnp.logical_not(mine))
    def _():
        pltpu.make_async_copy(cells, cells, send_sem.at[4]).wait()


def body(alm, legendre, order_of_slot):
    hbm = pl.BlockSpec(memory_space=pltpu.HBM)
    vmem = pl.BlockSpec(memory_space=pltpu.VMEM)
    narrow, twid = tables()
    operands = (alm, legendre, order_of_slot.reshape(8, 128), jnp.asarray(narrow), jnp.asarray(twid))
    operands = [pltpu.with_memory_space_constraint(x, pltpu.HBM) for x in operands]
    found = pl.pallas_call(
        kernel,
        out_shape=(
            jax.ShapeDtypeStruct((16, 512), F32),
            jax.ShapeDtypeStruct((16, 2, 128), F32),
        ),
        in_specs=[hbm] * 5,
        out_specs=(vmem, vmem),
        scratch_shapes=scratch_list()
        + [
            pltpu.SemaphoreType.DMA((8,)),
            pltpu.SemaphoreType.DMA((5,)),
            pltpu.SemaphoreType.DMA((5,)),
            pltpu.SemaphoreType.DMA((NT,)),
            pltpu.SemaphoreType.REGULAR((3,)),
        ],
        compiler_params=pltpu.CompilerParams(
            collective_id=0, has_side_effects=True, vmem_limit_bytes=48 * 1024 * 1024
        ),
    )(*operands)
    return pl.pallas_call(
        hand_on,
        out_shape=(
            jax.ShapeDtypeStruct((16, 512), F32),
            jax.ShapeDtypeStruct((16, 2, 128), F32),
        ),
        in_specs=[vmem] * 2,
        out_specs=(pl.BlockSpec(memory_space=pltpu.HBM),) * 2,
        scratch_shapes=[pltpu.SemaphoreType.DMA((2,))],
    )(*[pltpu.with_memory_space_constraint(x, pltpu.VMEM) for x in found])


def hand_on(map_i, alm_i, map_o, alm_o, sem):
    copies = [
        pltpu.make_async_copy(map_i, map_o, sem.at[0]),
        pltpu.make_async_copy(alm_i, alm_o, sem.at[1]),
    ]
    for copy in copies:
        copy.start()
    for copy in copies:
        copy.wait()


def solution(mesh):
    placed = (P("band", None, None, "tile"), P("band", "tile", None), P())
    return jax.shard_map(
        body,
        mesh=mesh,
        in_specs=placed,
        out_specs=(P("band", "tile"), P("band", None, "tile")),
        check_vma=False,
    )
```

```python
import math

import jax
import jax.numpy as jnp
import numpy as np
from jax import lax
from jax.experimental import pallas as pl
from jax.experimental.pallas import tpu as pltpu
from jax.sharding import PartitionSpec as P

C = 9
HALO = 32
RIDGE = 0.1
EPSILON = 1e-06
NB = 64
NT = 8
F32 = jnp.float32
BF16 = jnp.bfloat16
MESH = pl.DeviceIdType.MESH


SCRATCH = {
    "alm_v": ((16, C, 2, 128), BF16),
    "leg_v": ((16, 128, 1024), BF16),
    "ord_v": ((8, 128), jnp.int32),
    "narrow": ((768, 128), BF16),
    "twid": ((128, 128), F32),
    "stage": ((NT, 288, 128), F32),
    "parts": ((NT, 288, 128), BF16),
    "heard": ((NT, 288, 128), BF16),
    "slot_s": ((NB, 3, 2, 128), BF16),
    "slot_r": ((NB, 3, 2, 128), BF16),
    "turned": ((384, 128), F32),
    "mixed": ((3, 128, 128), F32),
    "modes": ((8, 48, 128), F32),
    "gathered": ((C, 32, 128), F32),
    "to_order": ((1024, 1024), BF16),
    "to_slot": ((1024, 1024), BF16),
    "maps": ((C, 64, 128), F32),
    "ahead": ((C, 64, 128), F32),
    "smoothed": ((45, 64, 128), F32),
    "ilc": ((64, 128), F32),
    "cells": ((64, 128), F32),
    "cells_r": ((64, 128), F32),
    "spec": ((128, 128), F32),
    "spec_s": ((16, 2, 128), BF16),
    "spec_r": ((NB, 2, 128), BF16),
    "spec_t": ((128, 128), F32),
    "every": ((NT, 32, 128), BF16),
    "sums": ((16, 32, 128), F32),
}


def scratch_list():
    return [pltpu.VMEM(shape, kind) for shape, kind in SCRATCH.values()]


def tables():
    xl, j, xs = np.meshgrid(np.arange(8), np.arange(2), np.arange(4), indexing="ij")
    xa, jr = (xl + 8 * xs).reshape(-1), j.reshape(-1)
    m0, m1 = np.arange(128), np.arange(8)
    ang = 2 * np.pi * ((xa[:, None] * m1[None, :]) % 32) / 32
    same = (jr[:, None, None] == np.arange(2)[None, None, :]).astype(np.float64)
    cs, sn = np.cos(ang)[:, :, None] * same, np.sin(ang)[:, :, None] * same
    real = np.stack([cs, -sn], axis=3).reshape(64, 32)
    imag = np.stack([sn, cs], axis=3).reshape(64, 32)
    first = np.concatenate([real, imag], axis=0)
    high = first.astype(BF16).astype(np.float64)
    first = np.concatenate([high, first - high], axis=1)
    ang = 2 * np.pi * (xa[:, None] * m0[None, :]) / 4096
    twiddle = np.stack([np.cos(ang), np.sin(ang)])
    ang = 2 * np.pi * ((m0[:, None] * m0[None, :]) % 128) / 128
    second = np.concatenate([np.cos(ang), -np.sin(ang)], axis=0) / 32
    back = np.concatenate([np.cos(ang), -np.sin(ang)], axis=1) / 32
    ang = 2 * np.pi * ((m1[:, None] * xa[None, :]) % 32) / 32
    same = (np.arange(2)[:, None, None] == jr[None, None, :]).astype(np.float64)
    cs, sn = np.cos(ang)[None] * same, np.sin(ang)[None] * same
    e0 = np.concatenate([cs, sn], axis=2).reshape(16, 128)
    e1 = np.concatenate([-sn, cs], axis=2).reshape(16, 128)
    none = np.zeros((48, 128))
    last = np.concatenate([e0, none, e1, none], axis=0)
    first = np.concatenate([first, np.zeros((128, 64))], axis=1)
    narrow = [first, second, back[:, :128], back[:, 128:], last]
    twiddle = np.concatenate([twiddle.reshape(128, 128), np.zeros((384, 128))], axis=0)
    return np.concatenate(narrow, axis=0).astype(BF16), twiddle.astype(np.float32)


def pair_table():
    return [(a, b) for a in range(C) for b in range(a, C)]


def window_sums(maps, smoothed):
    sub = lax.broadcasted_iota(jnp.int32, (8, 128), 0) % 4
    below = [jnp.where(sub >= k, 1.0, 0.0).astype(F32) for k in (1, 2, 3)]
    above = [jnp.where(sub <= 3 - k, 1.0, 0.0).astype(F32) for k in (1, 2, 3)]
    for at, (a, b) in enumerate(pair_table()):
        prod = [
            maps[a, 8 * i : 8 * i + 8, :] * maps[b, 8 * i : 8 * i + 8, :] for i in range(8)
        ]
        pre, post = [prod[0]], [prod[7]]
        for i in range(1, 8):
            pre.append(pre[-1] + prod[i])
            post.append(post[-1] + prod[7 - i])
        post = post[::-1]
        seg = pre[7]
        low = high = None
        for k in (1, 2, 3):
            down = below[k - 1] * pltpu.roll(seg, k, 0)
            up = above[k - 1] * pltpu.roll(seg, 8 - k, 0)
            low = down if low is None else low + down
            high = up if high is None else high + up
        base = high + pltpu.roll(seg + low + high, 127, 1) + pltpu.roll(low, 126, 1)
        for i in range(8):
            smoothed[at, 8 * i : 8 * i + 8, :] = post[i] + base + pltpu.roll(pre[i], 126, 1)


def solve_cells(ahead, smoothed, out):
    index = {}
    for at, (a, b) in enumerate(pair_table()):
        index[a, b] = at

    def step(i, _):
        rows = pl.ds(pl.multiple_of(i * 8, 8), 8)
        left = {key: smoothed[at, rows, :] for key, at in index.items()}
        trace = left[0, 0]
        for c in range(1, C):
            trace = trace + left[c, c]
        ridge = RIDGE * (trace * (1.0 / C) + EPSILON * (2 * HALO + 1))
        for c in range(C):
            left[c, c] = left[c, c] + ridge
        ones = [jnp.ones((8, 128), F32) for _ in range(C)]
        vals = [ahead[c, rows, :] for c in range(C)]
        top = bottom = None
        for k in range(C):
            inverse = 1.0 / left[k, k]
            scaled = ones[k] * inverse
            add_b, add_t = scaled * ones[k], scaled * vals[k]
            bottom = add_b if bottom is None else bottom + add_b
            top = add_t if top is None else top + add_t
            for r in range(k + 1, C):
                ratio = left[k, r] * inverse
                for q in range(r, C):
                    left[r, q] = left[r, q] - ratio * left[k, q]
                ones[r] = ones[r] - ratio * ones[k]
                vals[r] = vals[r] - ratio * vals[k]
        out[rows, :] = top / bottom
        return 0

    lax.fori_loop(0, 8, step, 0, unroll=8)


def band_peer(d, b):
    k, i = lax.div(d, 4), lax.rem(d, 4)
    dz = lax.rem(24 + (1 - 2 * lax.rem(k, 2)) * lax.div(k + 1, 2), 16)
    x = lax.rem(lax.div(b, 32) + lax.div(i, 2) + 1, 2)
    z = lax.rem(lax.rem(lax.div(b, 2), 16) + dz, 16)
    core = lax.rem(lax.rem(b, 2) + lax.rem(i, 2) + 1, 2)
    return (x * 16 + z) * 2 + core


def along_z(b, dz):
    z = lax.rem(lax.rem(lax.div(b, 2), 16) + dz, 16)
    return (lax.div(b, 32) * 16 + z) * 2 + lax.rem(b, 2)


def same_z(b, i):
    x = lax.rem(lax.div(b, 32) + i // 2, 2)
    return (x * 16 + lax.rem(lax.div(b, 2), 16)) * 2 + lax.rem(lax.rem(b, 2) + i % 2, 2)


FAR_FIRST = ((2, 1), (1, 1), (3, 1), (2, 0), (0, 1), (1, 0), (3, 0))


def tile_peer(t, dy, dx):
    return 2 * lax.rem(lax.div(t, 2) + dy, 4) + lax.rem(lax.rem(t, 2) + dx, 2)


def turn(block):
    return jnp.transpose(block, (1, 0))


def kernel(
    alm_h, leg_h, ord_h, narrow_h, twid_h,
    map_o, alm_o,
    alm_v, leg_v, ord_v, narrow, twid,
    stage, parts, heard, slot_s, slot_r, turned, mixed, modes, gathered, to_order, to_slot,
    maps, ahead, smoothed, ilc, cells, cells_r, spec, spec_s, spec_r, spec_t, every, sums,
    load_sem, send_sem, recv_sem, tile_sem, greet_sem,
):
    b = lax.axis_index("band")
    t = lax.axis_index("tile")
    owner_band = 8 * t + lax.div(b, 8)
    lane = lax.broadcasted_iota(jnp.int32, (8, 128), 1)

    loads = []
    for at, (src, dst) in enumerate(
        [(alm_h, alm_v)]
        + [(leg_h.at[pl.ds(4 * k, 4)], leg_v.at[pl.ds(4 * k, 4)]) for k in range(4)]
        + [(ord_h, ord_v), (narrow_h, narrow), (twid_h.at[pl.ds(0, 128)], twid)]
    ):
        copy = pltpu.make_async_copy(src, dst, load_sem.at[at])
        copy.start()
        loads.append(copy)

    bar = pltpu.get_barrier_semaphore()

    def greet(sem, others):
        for band, tile in others:
            pl.semaphore_signal(
                sem, inc=1, device_id={"band": band, "tile": tile}, device_id_type=MESH
            )

    greet(bar, [(b, tile_peer(t, dy, dx)) for dy, dx in FAR_FIRST])
    greet(bar, [(along_z(b, dz), t) for dz in (2, 14, 1, 15)])
    greet(bar, [(same_z(b, i), t) for i in (3, 2, 1)])

    loads[0].wait()
    for k in range(4):
        loads[1 + k].wait()
        for s in range(4 * k, 4 * k + 4):
            left = alm_v[s].reshape(18, 128)
            out = jnp.dot(left, leg_v[s], preferred_element_type=F32)
            for q in range(NT):
                stage[q, pl.ds(s, 18, stride=16), :] = out[:, 128 * q : 128 * q + 128]
    for q in range(NT):
        parts[q] = stage[q].astype(BF16)

    pl.semaphore_wait(bar, 14)
    greet(greet_sem.at[0], [(along_z(b, dz), t) for dz in (2, 14)])

    for dy, dx in FAR_FIRST:
        other = tile_peer(t, dy, dx)
        pltpu.make_async_remote_copy(
            src_ref=parts.at[other], dst_ref=heard.at[t], send_sem=send_sem.at[0],
            recv_sem=recv_sem.at[0], device_id={"band": b, "tile": other}, device_id_type=MESH,
        ).start()
    pltpu.make_async_copy(parts.at[t], heard.at[t], recv_sem.at[0]).start()

    for copy in loads[5:]:
        copy.wait()
    orders = ord_v[...].astype(F32)
    cols = turn(jnp.concatenate([orders, jnp.zeros((120, 128), F32)], axis=0))
    turned[0:128, :] = cols
    wide = lax.broadcasted_iota(jnp.int32, (8, 1024), 1).astype(F32)
    for s in range(16):
        pick = turned[pl.ds(s, 8, stride=16), :]
        for h in range(0, 8, 2):
            rows = [
                jnp.where(pick[:, k : k + 1] == wide, 1.0, 0.0) for k in (h, h + 1)
            ]
            to_order[s * 64 + h * 8 : s * 64 + h * 8 + 16, :] = jnp.concatenate(
                rows, axis=0
            ).astype(BF16)
    pl.semaphore_wait(greet_sem.at[0], 2)
    greet(greet_sem.at[1], [(along_z(b, dz), t) for dz in (4, 12)])
    orders = ord_v[...].astype(F32)
    tall = lax.broadcasted_iota(jnp.int32, (128, 128), 0).astype(F32)
    for h in range(8):
        row = jnp.broadcast_to(orders[h : h + 1, :], (128, 128))
        for k in range(8):
            to_slot[128 * k : 128 * k + 128, 128 * h : 128 * h + 128] = jnp.where(
                row == tall + 128.0 * k, 1.0, 0.0
            ).astype(BF16)

    pl.semaphore_wait(greet_sem.at[1], 2)
    greet(greet_sem.at[2], [(same_z(b, i), t) for i in (3, 2, 1)])
    pltpu.make_async_copy(heard, heard, recv_sem.at[0]).wait()
    total = heard[0].astype(F32)
    for q in range(1, NT):
        total = total + heard[q].astype(F32)
    total = jnp.concatenate([total, jnp.zeros((96, 128), F32)], axis=0)
    for k in range(3):
        block = turn(total[128 * k : 128 * k + 128])
        slot_s[:, k] = block.astype(BF16).reshape(NB, 2, 128)

    def send_slots(d, _):
        other = band_peer(d, b)
        pltpu.make_async_remote_copy(
            src_ref=slot_s.at[other], dst_ref=slot_r.at[b], send_sem=send_sem.at[1],
            recv_sem=recv_sem.at[1], device_id={"band": other, "tile": t}, device_id_type=MESH,
        ).start()
        return 0

    pl.semaphore_wait(greet_sem.at[2], 3)
    lax.fori_loop(0, NB - 1, send_slots, 0)
    pltpu.make_async_copy(slot_s.at[b], slot_r.at[b], recv_sem.at[1]).start()
    pltpu.make_async_copy(slot_r, slot_r, recv_sem.at[1]).wait()

    for k in range(3):
        mixed[k] = slot_r[:, k].astype(F32).reshape(128, 128)
    for k in range(3):
        block = [mixed[k, pl.ds(j, 64, stride=2), :] for j in range(2)]
        turned[128 * k : 128 * k + 128, :] = turn(jnp.concatenate(block, axis=0))
    lane24 = lax.broadcasted_iota(jnp.int32, (24, 128), 1)
    pieces = []
    for p in range(8):
        even = turned[pl.ds(2 * p, 24, stride=16), :]
        odd = turned[pl.ds(2 * p + 1, 24, stride=16), :]
        first_r = jnp.where(lane24 < 64, even, pltpu.roll(odd, 64, 1))
        second_r = jnp.where(lane24 < 64, pltpu.roll(even, 64, 1), odd)
        pieces.append(jnp.concatenate([first_r, second_r], axis=0).astype(BF16))
    ordered = jnp.dot(
        jnp.concatenate(pieces, axis=1), to_order[...], preferred_element_type=F32
    )
    for k in range(8):
        modes[k] = ordered[:, 128 * k : 128 * k + 128]
    for c in range(C):
        for k in range(8):
            gathered[c, 4 * k : 4 * k + 2, :] = modes[k, 2 * c : 2 * c + 2, :]
            gathered[c, 4 * k + 2 : 4 * k + 4, :] = modes[k, 24 + 2 * c : 26 + 2 * c, :]

    twr, twi = twid[0:64, :], twid[64:128, :]
    rows = []
    for c in range(C):
        data = gathered[c].astype(BF16)
        grid = jnp.dot(
            narrow[0:128, 0:64], jnp.concatenate([data, data], axis=0), preferred_element_type=F32
        )
        re, im = grid[:64], grid[64:]
        both = jnp.concatenate([re * twr - im * twi, re * twi + im * twr], axis=1)
        rows.append(both.astype(BF16))
    whole = jnp.dot(
        jnp.concatenate(rows, axis=0), narrow[128:384, :], preferred_element_type=F32
    )
    for c in range(C):
        found = whole[64 * c : 64 * c + 64].astype(BF16).astype(F32)
        maps[c] = found
        ahead[c] = pltpu.roll(found, 127, 1)

    window_sums(maps, smoothed)
    solve_cells(ahead, smoothed, ilc)
    ilc[...] = pltpu.roll(ilc[...], 1, 1)

    twr, twi = twid[0:64, :], twid[64:128, :]
    low = ilc[...].astype(BF16)
    re = jnp.dot(low, narrow[384:512, :], preferred_element_type=F32)
    im = jnp.dot(low, narrow[512:640, :], preferred_element_type=F32)
    both = jnp.concatenate([re * twr + im * twi, im * twr - re * twi], axis=0)
    spec[...] = jnp.dot(narrow[640:768, :], both.astype(BF16), preferred_element_type=F32)
    flat = jnp.concatenate([spec[pl.ds(k, 16, stride=8), :] for k in range(8)], axis=1)
    placed = jnp.dot(flat.astype(BF16), to_slot[...], preferred_element_type=F32)
    half = lax.broadcasted_iota(jnp.int32, (8, 128), 1) < 64
    for k in range(8):
        e0, e1 = (placed[8 * e : 8 * e + 8, 128 * k : 128 * k + 128] for e in range(2))
        low = jnp.where(half, e0, pltpu.roll(e1, 64, 1))
        high = jnp.where(half, pltpu.roll(e0, 64, 1), e1)
        spec_s[2 * k] = low[0:2].astype(BF16)
        spec_s[2 * k + 1] = high[0:2].astype(BF16)
    def send_spectra(d, _):
        other = band_peer(d, b)
        pltpu.make_async_remote_copy(
            src_ref=spec_s.at[lax.div(other, 4)], dst_ref=spec_r.at[b], send_sem=send_sem.at[2],
            recv_sem=recv_sem.at[2], device_id={"band": other, "tile": t}, device_id_type=MESH,
        ).start()
        return 0

    lax.fori_loop(0, NB - 1, send_spectra, 0)
    pltpu.make_async_copy(spec_s.at[lax.div(b, 4)], spec_r.at[b], recv_sem.at[2]).start()

    lines = jnp.concatenate(
        [ilc[pl.ds(k, 8, stride=8), :] for k in range(8)] + [jnp.zeros((64, 128), F32)], axis=0
    )
    turned[0:128, :] = turn(lines)
    lane32 = lax.broadcasted_iota(jnp.int32, (32, 128), 1)
    for j in range(2):
        line = None
        for k in range(4):
            part = turned[pl.ds(k, 32, stride=4), :]
            part = pltpu.roll(part, (32 * k - 32 * j) % 128, 1) if k != j else part
            keep = jnp.logical_and(lane32 >= 32 * k, lane32 < 32 * k + 32)
            part = jnp.where(keep, part, 0.0)
            line = part if line is None else line + part
        cells[pl.ds(j, 32, stride=2), :] = line
    place = pl.ds(pl.multiple_of(8 * lax.rem(b, 8), 8), 8)
    for q in range(NT):
        own = jnp.logical_and(owner_band == b, t == q)

        @pl.when(own)
        def _():
            pltpu.make_async_copy(
                cells.at[8 * q : 8 * q + 8], cells_r.at[place], recv_sem.at[4]
            ).start()

        @pl.when(jnp.logical_not(own))
        def _():
            pltpu.make_async_remote_copy(
                src_ref=cells.at[8 * q : 8 * q + 8], dst_ref=cells_r.at[place],
                send_sem=send_sem.at[4], recv_sem=recv_sem.at[4],
                device_id={"band": owner_band, "tile": q}, device_id_type=MESH,
            ).start()

    pltpu.make_async_copy(spec_r, spec_r, recv_sem.at[2]).wait()
    spec_t[...] = turn(spec_r[...].astype(F32).reshape(128, 128))
    start = 16 * lax.rem(b, 4)
    own_s = [spec_t[pl.ds(pl.multiple_of(64 * e + start, 16), 16), :] for e in range(2)]
    every[t] = jnp.concatenate(own_s, axis=0).astype(BF16)
    for dy, dx in FAR_FIRST:
        other = tile_peer(t, dy, dx)
        pltpu.make_async_remote_copy(
            src_ref=every.at[t], dst_ref=every.at[t], send_sem=send_sem.at[3],
            recv_sem=tile_sem.at[t], device_id={"band": b, "tile": other}, device_id_type=MESH,
        ).start()
    for at, (dy, dx) in enumerate(((0, 0),) + FAR_FIRST[::-1]):
        other = tile_peer(t, dy, dx)
        if at == NT - 1:
            pltpu.make_async_copy(cells_r, cells_r, recv_sem.at[4]).wait()
            for q in range(4):
                for j in range(2):
                    ilc[pl.ds(16 * q + j, 8, stride=2), :] = cells_r[pl.ds(2 * q + j, 8, stride=8), :]
                map_o[:, 128 * q : 128 * q + 128] = ilc[16 * q : 16 * q + 16, :]
        if at:
            pltpu.make_async_copy(every.at[other], every.at[other], tile_sem.at[other]).wait()
        block = every[other]
        cycles = pl.ds(pl.multiple_of(128 * other, 128), 128)
        for s in range(16):
            out = lax.dot_general(
                block, leg_v[s, :, cycles], (((1,), (1,)), ((), ())), preferred_element_type=F32
            )
            if at == 0:
                sums[s] = out
            elif at < NT - 1:
                sums[s] += out
            else:
                out = out + sums[s]
                alm_o[s, 0:1, :] = out[s : s + 1]
                alm_o[s, 1:2, :] = out[16 + s : 17 + s]

    sent = parts.at[pl.ds(0, NT - 1)]
    pltpu.make_async_copy(sent, sent, send_sem.at[0]).wait()
    sent = slot_s.at[pl.ds(0, NB - 1)]
    pltpu.make_async_copy(sent, sent, send_sem.at[1]).wait()
    sent = spec_r.at[pl.ds(0, NB - 1)]
    pltpu.make_async_copy(sent, sent, send_sem.at[2]).wait()
    sent = every.at[pl.ds(0, NT - 1)]
    pltpu.make_async_copy(sent, sent, send_sem.at[3]).wait()
    mine = owner_band == b

    @pl.when(mine)
    def _():
        sent = cells.at[0:56]
        pltpu.make_async_copy(sent, sent, send_sem.at[4]).wait()

    @pl.when(jnp.logical_not(mine))
    def _():
        pltpu.make_async_copy(cells, cells, send_sem.at[4]).wait()


def body(alm, legendre, order_of_slot):
    hbm = pl.BlockSpec(memory_space=pltpu.HBM)
    vmem = pl.BlockSpec(memory_space=pltpu.VMEM)
    narrow, twid = tables()
    operands = (alm, legendre, order_of_slot.reshape(8, 128), jnp.asarray(narrow), jnp.asarray(twid))
    operands = [pltpu.with_memory_space_constraint(x, pltpu.HBM) for x in operands]
    found = pl.pallas_call(
        kernel,
        out_shape=(
            jax.ShapeDtypeStruct((16, 512), F32),
            jax.ShapeDtypeStruct((16, 2, 128), F32),
        ),
        in_specs=[hbm] * 5,
        out_specs=(vmem, vmem),
        scratch_shapes=scratch_list()
        + [
            pltpu.SemaphoreType.DMA((8,)),
            pltpu.SemaphoreType.DMA((5,)),
            pltpu.SemaphoreType.DMA((5,)),
            pltpu.SemaphoreType.DMA((NT,)),
            pltpu.SemaphoreType.REGULAR((3,)),
        ],
        compiler_params=pltpu.CompilerParams(
            collective_id=0, has_side_effects=True, vmem_limit_bytes=48 * 1024 * 1024
        ),
    )(*operands)
    return pl.pallas_call(
        hand_on,
        out_shape=(
            jax.ShapeDtypeStruct((16, 512), F32),
            jax.ShapeDtypeStruct((16, 2, 128), F32),
        ),
        in_specs=[vmem] * 2,
        out_specs=(pl.BlockSpec(memory_space=pltpu.HBM),) * 2,
        scratch_shapes=[pltpu.SemaphoreType.DMA((2,))],
    )(*[pltpu.with_memory_space_constraint(x, pltpu.VMEM) for x in found])


def hand_on(map_i, alm_i, map_o, alm_o, sem):
    copies = [
        pltpu.make_async_copy(map_i, map_o, sem.at[0]),
        pltpu.make_async_copy(alm_i, alm_o, sem.at[1]),
    ]
    for copy in copies:
        copy.start()
    for copy in copies:
        copy.wait()


def solution(mesh):
    placed = (P("band", None, None, "tile"), P("band", "tile", None), P())
    return jax.shard_map(
        body,
        mesh=mesh,
        in_specs=placed,
        out_specs=(P("band", "tile"), P("band", None, "tile")),
        check_vma=False,
    )
```
